32 devices in a mesh: img: 16 (over z, y, x), lat: 2 (over core).
Axes of the slice: x: 2, y: 2, z: 4, core: 2. Of those that a mesh axis runs over, the one named last changes fastest.
Arguments:
- media_tokens: bfloat16 [80, 256, 1024], P('img', 'lat'), may hold values from -6 to 6
- image_counts: int32 [16], P('img'), may hold values from 1 to 5
- latent_init: bfloat16 [64, 1024], P('lat'), may hold values from -6 to 6
- cotangent: bfloat16 [80, 64, 1024], P('img', 'lat'), may hold values from -6 to 6
- query_weight: bfloat16 [2, 1024, 512], P(None, ('img', 'lat')), may hold values from -0.1875 to 0.1875
- key_value_weight: bfloat16 [2, 1024, 1024], P(None, ('img', 'lat')), may hold values from -0.1875 to 0.1875
- output_weight: bfloat16 [2, 512, 1024], P(None, ('img', 'lat')), may hold values from -0.75 to 0.75
- up_weight: bfloat16 [2, 1024, 4096], P(None, ('img', 'lat')), may hold values from -0.1875 to 0.1875
- down_weight: bfloat16 [2, 4096, 1024], P(None, ('img', 'lat')), may hold values from -0.09375 to 0.09375
- norm_gain: bfloat16 [2, 3, 1024], P(None, None, ('img', 'lat')), may hold values from 0.5 to 1.5
- norm_shift: bfloat16 [2, 3, 1024], P(None, None, ('img', 'lat')), may hold values from -1.75 to 1.75
Outputs:
- resampled: float32 [80, 64, 1024], P('img', 'lat')
- media_grad: float32 [80, 256, 1024], P('img', 'lat')
- latent_grad: float32 [64, 1024], P('lat')
- query_grad: float32 [2, 1024, 512], P(None, ('img', 'lat'))
- key_value_grad: float32 [2, 1024, 1024], P(None, ('img', 'lat'))
- output_grad: float32 [2, 512, 1024], P(None, ('img', 'lat'))
- up_grad: float32 [2, 1024, 4096], P(None, ('img', 'lat'))
- down_grad: float32 [2, 4096, 1024], P(None, ('img', 'lat'))
- gain_grad: float32 [2, 3, 1024], P(None, None, ('img', 'lat'))
- shift_grad: float32 [2, 3, 1024], P(None, None, ('img', 'lat'))
The draws below stay inside these ranges and needn't reach their ends.
Inputs may be any that keep to these rules, and one draw needn't show every extreme that they name: image_counts[b] is the number of sample b's 5 slots that hold an image: slot j of it is filled when j < image_counts[b], the rest are padding.
All inputs are finite; a program needn't handle non-finite values.
Results may differ from the reference program's by a relative error of at most 0.019.
Values may be sent and summed in bfloat16 or wider, within the bound.
No kernel may reach another device: no remote copies, remote signals or barrier semaphores. Data moves between devices by JAX's collectives and lax.ppermute only.
A program may use at most 320 MiB of HBM per device.

```python
import jax
import jax.numpy as jnp
from jax import lax

D = 1024
HEADS = 8
HEAD = 64
INNER = 512
FF = 4096
LATENTS = 64
PATCHES = 256
MEDIA = 5
LAYERS = 2
SAMPLES = 16
SLOTS = 80


def with_ends(array, stream_key, low, largest):
    place = [jax.random.randint(jax.random.fold_in(stream_key, axis), (), 0, length) for axis, length in enumerate(array.shape)]
    widest = array.shape.index(max(array.shape))
    beside = place[:widest] + [(place[widest] + 1) % array.shape[widest]] + place[widest + 1:]
    return array.at[tuple(place)].set(low).at[tuple(beside)].set(largest)


def levels(key, extent, shards, least, largest):
    def one(position, blocks):
        heights = jax.random.uniform(jax.random.fold_in(jax.random.fold_in(key, 6), position), (blocks,), jnp.float32, least / len(shards), largest / len(shards))
        return jnp.repeat(jnp.exp(heights), extent[position] // blocks).reshape((-1,) + (1,) * (len(extent) - position - 1))

    gain = one(*shards[0])
    for cut in shards[1:]:
        gain = gain * one(*cut)
    return gain


def centred(rng, shape, scale, bound, shards=(), kind=jnp.bfloat16):
    entries = scale * jax.random.normal(rng, shape, jnp.float32)
    if shards:
        entries = entries * levels(rng, shape, shards, -0.22, 0.18)
    return jnp.clip(entries, -bound, bound).astype(kind)


def setup_inputs(seed: int = 0) -> dict:
    key_list = jax.random.split(jax.random.key(seed), 12)
    return {
        "media_tokens": centred(key_list[0], (SLOTS, PATCHES, D), 1.0, 6.0, ((0, 16), (1, 2))),
        "image_counts": with_ends(jax.random.randint(key_list[1], (SAMPLES,), 1, MEDIA + 1), jax.random.fold_in(key_list[1], 1), 1, MEDIA).astype(jnp.int32),
        "latent_init": centred(key_list[2], (LATENTS, D), 1.0, 6.0, ((0, 2),)),
        "cotangent": centred(key_list[3], (SLOTS, LATENTS, D), 1.0, 6.0, ((0, 16), (1, 2))),
        "query_weight": centred(key_list[4], (LAYERS, D, INNER), D ** -0.5, 0.1875, ((1, 32),)),
        "key_value_weight": centred(key_list[5], (LAYERS, D, 2 * INNER), D ** -0.5, 0.1875, ((1, 32),)),
        "output_weight": centred(key_list[6], (LAYERS, INNER, D), (INNER // 8) ** -0.5, 0.75, ((1, 32),)),
        "up_weight": centred(key_list[7], (LAYERS, D, FF), D ** -0.5, 0.1875, ((1, 32),)),
        "down_weight": centred(key_list[8], (LAYERS, FF, D), FF ** -0.5, 0.09375, ((1, 32),)),
        "norm_gain": jnp.clip(1.0 + 0.1 * jax.random.normal(key_list[9], (LAYERS, 3, D), jnp.float32), 0.5, 1.5).astype(jnp.bfloat16),
        "norm_shift": centred(key_list[10], (LAYERS, 3, D), 0.3, 1.75, ((2, 32),)),
    }


@jax.custom_vjp
def low(v):
    return lax.optimization_barrier(v.astype(jnp.bfloat16)).astype(jnp.float32)

@jax.custom_vjp
def low_back(v):
    return v

def low_keep(v):
    return (low(v), None)

def low_pass(kept, grad):
    return (grad,)

def back_keep(v):
    return (v, None)

def back_low(kept, grad):
    return (low(grad),)
low.defvjp(low_keep, low_pass)
low_back.defvjp(back_keep, back_low)
highest = lax.Precision.HIGHEST

def norm_rows(inputs, scale_row, shift_row):
    average = lax.optimization_barrier(jnp.mean(inputs, axis=-1, keepdims=True))
    centered = inputs - average
    variance = lax.optimization_barrier(jnp.mean(centered * centered, axis=-1, keepdims=True))
    return centered * lax.rsqrt(variance + 1e-05) * scale_row + shift_row

def project(inputs, matrix):
    return jnp.einsum('...d,de->...e', inputs, matrix, precision=highest)

def one_layer(latent_rows, media_rows, query_projection_weight, key_value_w, output_projection_weight, up_projection_weight, down_projection_weight, gains, shifts):
    media_norm = low(norm_rows(media_rows, gains[0], shifts[0]))
    normed_latent_rows = low(norm_rows(latent_rows, gains[1], shifts[1]))
    query = low_back(low(project(normed_latent_rows, query_projection_weight)))
    joined = jnp.concatenate([media_norm, normed_latent_rows], axis=1)
    key_value = low_back(low(project(joined, key_value_w)))
    slot_count = query.shape[0]
    query_rows = query.shape[1]
    key_rows = joined.shape[1]
    query_heads = query.reshape(slot_count, query_rows, HEADS, HEAD)
    key_heads = key_value[..., :INNER].reshape(slot_count, key_rows, HEADS, HEAD)
    value_heads = key_value[..., INNER:].reshape(slot_count, key_rows, HEADS, HEAD)
    scores = low_back(jnp.einsum('sqhe,skhe->shqk', query_heads, key_heads, precision=highest) * 0.125)
    probs = low(jax.nn.softmax(scores, axis=-1))
    mixed_rows = jnp.einsum('shqk,skhe->sqhe', probs, value_heads, precision=highest)
    mixed_rows = low_back(low(mixed_rows.reshape(slot_count, query_rows, INNER)))
    residual_after = latent_rows + low_back(project(mixed_rows, output_projection_weight))
    normalized_rows = low(norm_rows(residual_after, gains[2], shifts[2]))
    hidden_rows = low_back(project(normalized_rows, up_projection_weight))
    activated_rows = low(jax.nn.gelu(hidden_rows, approximate=False))
    return residual_after + low_back(project(activated_rows, down_projection_weight))

def forward(media_all, latent_rows, query_projection_weight, key_value_w, output_projection_weight, up_projection_weight, down_projection_weight, gains, shifts, valid_mask):
    media_blocks = media_all.reshape(SAMPLES, MEDIA, PATCHES, D)

    def per_sample(pair):
        block, keep_slot = pair
        current = jnp.broadcast_to(latent_rows, (MEDIA, LATENTS, D))
        for level_index in range(LAYERS):
            current = one_layer(current, block, query_projection_weight[level_index], key_value_w[level_index], output_projection_weight[level_index], up_projection_weight[level_index], down_projection_weight[level_index], gains[level_index], shifts[level_index])
        return current * keep_slot[:, None, None]
    layer_result = lax.map(jax.checkpoint(per_sample), (media_blocks, valid_mask))
    return layer_result.reshape(SLOTS, LATENTS, D)

def reference(media_tokens, image_counts, latent_init, cotangent, query_weight, key_value_weight, output_weight, up_weight, down_weight, norm_gain, norm_shift):
    valid_mask = (jnp.arange(MEDIA)[None, :] < image_counts[:, None]).astype(jnp.float32)
    inputs = (media_tokens.astype(jnp.float32), latent_init.astype(jnp.float32), query_weight.astype(jnp.float32), key_value_weight.astype(jnp.float32), output_weight.astype(jnp.float32), up_weight.astype(jnp.float32), down_weight.astype(jnp.float32), norm_gain.astype(jnp.float32), norm_shift.astype(jnp.float32))

    def whole(media_all, latent_rows, query_projection_weight, key_value_w, output_projection_weight, up_projection_weight, down_projection_weight, gains, shifts):
        return forward(media_all, latent_rows, query_projection_weight, key_value_w, output_projection_weight, up_projection_weight, down_projection_weight, gains, shifts, valid_mask)
    resampled, pullback = jax.vjp(whole, *inputs)
    grads = pullback(cotangent.astype(jnp.float32))
    return (resampled, grads[0], grads[1], grads[2], grads[3], grads[4], grads[5], grads[6], grads[7], grads[8])
```

```python
import jax
import jax.numpy as jnp
from jax import lax
from jax.sharding import PartitionSpec as P

HEAD = 64
MEDIA = 5
LAYERS = 2
F32 = jnp.float32
BF16 = jnp.bfloat16


class Bit:
    def __init__(self, axis, size, place, rank):
        self.rank = rank
        self.axis = axis
        self.mask = 1 << place
        self.pairs = [(source, source ^ self.mask) for source in range(size)]

    def mine(self):
        return (lax.axis_index(self.axis) // self.mask) % 2

    def swap(self, array):
        return lax.ppermute(array, self.axis, self.pairs)


class Layout:
    def __init__(self, img, lat):
        lat_bits = [Bit("lat", lat, k, k) for k in range(lat.bit_length() - 1)]
        img_bits = [Bit("img", img, k, k + len(lat_bits)) for k in range(img.bit_length() - 1)]
        self.devices = img * lat
        self.lat = lat_bits
        self.img = img_bits
        self.first, self.second = img_bits[0], img_bits[1]
        self.tensor_img = img_bits[2]
        self.far = list(reversed(img_bits[3:]))
        self.tensor = [self.tensor_img] + list(reversed(lat_bits))
        self.split = 2 ** len(self.tensor)


def join(array, order, have):
    have = list(have)
    for bit in order:
        other = bit.swap(array)
        low = bit.mine() == 0
        place = sum(1 for held in have if held.rank > bit.rank)
        array = jnp.stack([jnp.where(low, array, other), jnp.where(low, other, array)], axis=place)
        have.insert(place, bit)
    return array, have


def part(array, bit, place, own):
    index = bit.mine() if own else 1 - bit.mine()
    return lax.dynamic_index_in_dim(array, index, place, keepdims=False)


def shed(array, order, have):
    have = list(have)
    for bit in order:
        place = have.index(bit)
        other = bit.swap(part(array, bit, place, False).astype(BF16))
        array = part(array, bit, place, True).astype(F32) + other.astype(F32)
        have.pop(place)
    return array, have


def all_sum(array, order):
    for bit in order:
        array = array + bit.swap(array)
    return array


def norm_rows(inputs, scale_row, shift_row):
    average = jnp.mean(inputs, axis=-1, keepdims=True)
    centered = inputs - average
    variance = jnp.mean(centered * centered, axis=-1, keepdims=True)
    return centered * lax.rsqrt(variance + 1e-05) * scale_row + shift_row


def mm(a, b):
    return lax.dot_general(a, b, (((1,), (0,)), ((), ())), preferred_element_type=F32)


def mm_nt(a, b):
    return lax.dot_general(a, b, (((1,), (1,)), ((), ())), preferred_element_type=F32)


def mm_tn(a, b):
    return lax.dot_general(a, b, (((0,), (0,)), ((), ())), preferred_element_type=F32)


class Weights:
    pass


def gather_attention(lay, kv_shard, out_shard, query_shard, extra):
    rows = kv_shard.shape[0]
    half = rows // 2
    query_pack = jnp.concatenate([query_shard[:half], query_shard[half:]], axis=1)
    parts = [kv_shard, out_shard, query_pack]
    if extra is not None:
        parts.append(extra)
    packed = jnp.concatenate(parts, axis=0)
    packed, have = join(packed, lay.far + [lay.tensor_img], [])
    left = packed[..., :rows, :]
    right = packed[..., rows:, :]
    left, left_have = join(left, [lay.first, lay.second], have)
    right, right_have = join(right, [lay.second, lay.first], have)
    left, _ = join(left, lay.lat, left_have)
    right, _ = join(right, lay.lat, right_have)
    width = kv_shard.shape[1]
    key_value = left.reshape(-1, width)
    right = right.reshape((lay.devices,) + right.shape[-2:])
    out_rows = out_shard.shape[0]
    output = right[:, :out_rows].reshape(-1, width)
    pack = right[:, out_rows : out_rows + half]
    query = jnp.concatenate([pack[..., : width // 2], pack[..., width // 2 :]], axis=1)
    query = query.reshape(-1, width // 2)
    if extra is None:
        return key_value, output, query, None
    norms = jnp.sum(right[:, out_rows + half :].astype(F32), axis=0)
    return key_value, output, query, norms


def feed_columns(lay, array, forward):
    width = array.shape[-1] // lay.devices if forward else None
    ranks = [bit.rank for bit in lay.tensor]
    owner = []
    for device in range(lay.devices):
        value = 0
        for rank in ranks:
            value = value * 2 + (device >> rank) % 2
        owner.append(value)
    if forward:
        blocks = [array[..., d * width : (d + 1) * width] for d in range(lay.devices)]
        sets = [
            jnp.concatenate([blocks[d] for d in range(lay.devices) if owner[d] == s], axis=-1)
            for s in range(lay.split)
        ]
        return jnp.stack(sets)
    width = array.shape[-1] * lay.split // lay.devices
    seen = [0] * lay.split
    blocks = []
    for device in range(lay.devices):
        s = owner[device]
        blocks.append(array[s, :, seen[s] * width : (seen[s] + 1) * width])
        seen[s] += 1
    return jnp.concatenate(blocks, axis=-1)


def exchange(array, bit, place):
    other = bit.swap(part(array, bit, place, False))
    own = part(array, bit, place, True)
    low = bit.mine() == 0
    return jnp.stack([jnp.where(low, own, other), jnp.where(low, other, own)], axis=place)


def gather_feed(lay, up_shard, down_shard):
    rows = up_shard.shape[0]
    width = down_shard.shape[1]
    columns = up_shard.shape[1] // lay.split
    up = feed_columns(lay, up_shard, True)
    up = up.reshape((2,) * len(lay.tensor) + (rows, columns))
    for place in reversed(range(len(lay.tensor))):
        up = exchange(up, lay.tensor[place], place)
    up, have = join(up, lay.far, lay.tensor)
    down, down_have = join(down_shard, lay.far, [])
    up, _ = join(up, [lay.first, lay.second], have)
    down, _ = join(down, [lay.second, lay.first], down_have)
    return up.reshape(-1, columns), down.reshape(-1, width)


def reduce_feed(lay, up_term, down_term, rows):
    columns = up_term.shape[1]
    width = down_term.shape[1]
    every = list(reversed(lay.lat + lay.img))
    have = [bit for bit in every]
    up = up_term.reshape((2,) * len(have) + (rows, columns))
    up, have = shed(up, [lay.second, lay.first], have)
    rest = [bit for bit in every if bit not in lay.tensor]
    down = down_term.reshape((2,) * len(rest) + (-1, width))
    down, rest = shed(down, [lay.first, lay.second], rest)
    far = list(reversed(lay.far))
    up, have = shed(up, far, have)
    down, rest = shed(down, far, rest)
    up = up.astype(BF16)
    for place in range(len(lay.tensor)):
        up = exchange(up, lay.tensor[place], place)
    up = feed_columns(lay, up.reshape(lay.split, rows, columns), False)
    return up.astype(F32), down


def reduce_attention(lay, key_value_term, output_term, query_term):
    width = key_value_term.shape[1]
    every = list(reversed(lay.lat + lay.img))
    rows = key_value_term.shape[0] // lay.devices
    half = rows // 2
    out_rows = output_term.shape[0] // lay.devices
    left = key_value_term.astype(BF16).reshape((2,) * len(every) + (rows, width))
    query = query_term.astype(BF16).reshape(lay.devices, 2, half, width // 2)
    query = jnp.concatenate([query[:, 0], query[:, 1]], axis=-1)
    right = jnp.concatenate(
        [output_term.astype(BF16).reshape(lay.devices, out_rows, width), query], axis=1
    )
    right = right.reshape((2,) * len(every) + (out_rows + half, width))
    left, left_have = shed(left, lay.lat, every)
    right, right_have = shed(right, lay.lat, every)
    left, left_have = shed(left, [lay.second, lay.first], left_have)
    right, right_have = shed(right, [lay.first, lay.second], right_have)
    packed = jnp.concatenate([left, right], axis=-2)
    packed, _ = shed(packed, [lay.tensor_img] + list(reversed(lay.far)), left_have)
    output = packed[rows : rows + out_rows]
    pack = packed[rows + out_rows :]
    query = jnp.concatenate([pack[:, : width // 2], pack[:, width // 2 :]], axis=0)
    return packed[:rows], output, query


def gather_rows(lay, rows):
    joined, _ = join(rows, lay.tensor, [])
    return joined.reshape(-1, rows.shape[-1])


def return_rows(lay, rows):
    array = rows.reshape((2,) * len(lay.tensor) + (-1, rows.shape[-1]))
    array, _ = shed(array, list(reversed(lay.tensor)), lay.tensor)
    return array


def layer_forward(lay, latent_rows, media_float, current):
    query_w, key_value_w, output_w, up_w, down_w, gain_rows, shift_rows = current
    inner_width = query_w.shape[1]
    head_count = inner_width // HEAD
    slot_count, query_rows, model = latent_rows.shape
    media_norm = norm_rows(media_float, gain_rows[0], shift_rows[0]).astype(BF16)
    normed_latent_rows = norm_rows(latent_rows, gain_rows[1], shift_rows[1]).astype(BF16)
    query = mm(normed_latent_rows.reshape(-1, model), query_w).astype(BF16)
    joined = jnp.concatenate([media_norm, normed_latent_rows], axis=1)
    own_pairs = mm(joined.reshape(-1, model), key_value_w).astype(BF16)
    own_pairs = own_pairs.reshape(slot_count, -1, 2 * inner_width)
    key_value, _ = join(own_pairs, lay.lat, [])
    key_value = jnp.concatenate([key_value[k] for k in range(key_value.shape[0])], axis=1)
    key_rows = key_value.shape[1]
    query_heads = query.reshape(slot_count, query_rows, head_count, HEAD)
    key_heads = key_value[..., :inner_width].reshape(slot_count, key_rows, head_count, HEAD)
    value_heads = key_value[..., inner_width:].reshape(slot_count, key_rows, head_count, HEAD)
    scores = (
        jnp.einsum("sqhe,skhe->shqk", query_heads, key_heads, preferred_element_type=F32) * 0.125
    )
    row_max = jnp.max(scores, axis=-1, keepdims=True)
    exponent = jnp.exp(scores - row_max)
    totals = jnp.sum(exponent, axis=-1, keepdims=True)
    probs = (exponent / totals).astype(BF16)
    log_total = row_max + jnp.log(totals)
    mixed_rows = jnp.einsum("shqk,skhe->sqhe", probs, value_heads, preferred_element_type=F32)
    mixed_rows = mixed_rows.reshape(-1, inner_width).astype(BF16)
    residual_after = latent_rows + mm(mixed_rows, output_w).reshape(latent_rows.shape)
    normalized_rows = norm_rows(residual_after, gain_rows[2], shift_rows[2]).astype(BF16)
    shared_rows = gather_rows(lay, normalized_rows.reshape(-1, model))
    hidden_rows = mm(shared_rows, up_w)
    activated_rows = jax.nn.gelu(hidden_rows, approximate=False).astype(BF16)
    branch = return_rows(lay, mm(activated_rows, down_w))
    layer_result = residual_after + branch.reshape(latent_rows.shape)
    stored = (
        latent_rows,
        joined,
        query_heads,
        key_heads,
        value_heads,
        log_total,
        mixed_rows,
        residual_after,
        shared_rows,
        hidden_rows,
        activated_rows,
    )
    return (layer_result, stored)


def layer_backward(lay, upstream, media_float, current, stored):
    query_w, key_value_w, output_w, up_w, down_w, gain_rows, shift_rows = current
    (
        latent_rows,
        joined,
        query_heads,
        key_heads,
        value_heads,
        log_total,
        mixed_rows,
        residual_after,
        shared_rows,
        hidden_rows,
        activated_rows,
    ) = stored
    inner_width = query_w.shape[1]
    slot_count, query_rows, model = latent_rows.shape
    patch_rows = media_float.shape[1]
    key_rows = key_heads.shape[1]
    head_count = inner_width // HEAD
    branch_gradient = gather_rows(lay, upstream.astype(BF16).reshape(-1, model))
    down_term = mm_tn(activated_rows, branch_gradient).astype(BF16)
    activated_grad = mm_nt(branch_gradient, down_w)
    _, gelu_pull = jax.vjp(lambda inputs: jax.nn.gelu(inputs, approximate=False), hidden_rows)
    hidden_grad = gelu_pull(activated_grad)[0].astype(BF16)
    up_term = mm_tn(shared_rows, hidden_grad).astype(BF16)
    normed_grad = return_rows(lay, mm_nt(hidden_grad, up_w)).reshape(upstream.shape)
    feed_grads = reduce_feed(lay, up_term, down_term, model // lay.devices)
    _, feed_pull = jax.vjp(norm_rows, residual_after, gain_rows[2], shift_rows[2])
    d_after, gain_feed, shift_feed = feed_pull(normed_grad)
    d_after = d_after + upstream
    attention_grad = d_after.astype(BF16).reshape(-1, model)
    output_term = mm_tn(mixed_rows, attention_grad)
    mixed_grad = mm_nt(attention_grad, output_w)
    mixed_grad = mixed_grad.astype(BF16).reshape(slot_count, query_rows, head_count, HEAD)
    scores = (
        jnp.einsum("sqhe,skhe->shqk", query_heads, key_heads, preferred_element_type=F32) * 0.125
    )
    soft = jnp.exp(scores - log_total)
    probs = soft.astype(BF16)
    d_probs = jnp.einsum("sqhe,skhe->shqk", mixed_grad, value_heads, preferred_element_type=F32)
    d_values = jnp.einsum("shqk,sqhe->skhe", probs, mixed_grad, preferred_element_type=F32)
    d_scores = soft * (d_probs - jnp.sum(d_probs * soft, axis=-1, keepdims=True))
    d_scores = d_scores.astype(BF16)
    query_input_grad = (
        jnp.einsum("shqk,skhe->sqhe", d_scores, key_heads, preferred_element_type=F32) * 0.125
    )
    query_input_grad = query_input_grad.reshape(-1, inner_width).astype(BF16)
    d_keys = (
        jnp.einsum("shqk,sqhe->skhe", d_scores, query_heads, preferred_element_type=F32) * 0.125
    )
    d_pairs = jnp.concatenate(
        [
            d_keys.reshape(slot_count, key_rows, inner_width),
            d_values.reshape(slot_count, key_rows, inner_width),
        ],
        axis=-1,
    )
    parts = 2 ** len(lay.lat)
    d_pairs = jnp.moveaxis(d_pairs.reshape(slot_count, parts, key_rows // parts, -1), 1, 0)
    own_pairs, _ = shed(d_pairs, lay.lat, lay.lat)
    own_pairs = own_pairs.astype(BF16).reshape(-1, 2 * inner_width)
    flat_joined = joined.reshape(-1, model)
    key_value_term = mm_tn(flat_joined, own_pairs)
    d_joined = mm_nt(own_pairs, key_value_w).reshape(joined.shape)
    normed_latent_rows = joined[:, patch_rows:].reshape(-1, model)
    query_term = mm_tn(normed_latent_rows, query_input_grad)
    attention_grads = reduce_attention(lay, key_value_term, output_term, query_term)
    d_latent_norm = d_joined[:, patch_rows:] + mm_nt(query_input_grad, query_w).reshape(
        latent_rows.shape
    )
    _, media_pull = jax.vjp(norm_rows, media_float, gain_rows[0], shift_rows[0])
    d_media, gain_media, shift_media = media_pull(d_joined[:, :patch_rows])
    _, latent_pull = jax.vjp(norm_rows, latent_rows, gain_rows[1], shift_rows[1])
    d_latent, gain_latent, shift_latent = latent_pull(d_latent_norm)
    d_rows = d_latent + d_after
    norm_terms = ([gain_media, gain_latent, gain_feed], [shift_media, shift_latent, shift_feed])
    return (d_rows, d_media, attention_grads, feed_grads, norm_terms)


def make_device(lay):
    def per_device(
        media_tokens,
        image_counts,
        latent_init,
        cotangent,
        query_weight,
        key_value_weight,
        output_weight,
        up_weight,
        down_weight,
        norm_gain,
        norm_shift,
    ):
        slot_count = media_tokens.shape[0]
        model_width = media_tokens.shape[2]
        latent_count = latent_init.shape[0]
        position = jnp.arange(slot_count) % MEDIA
        per_slot = jnp.repeat(image_counts, MEDIA)
        valid_mask = (position < per_slot).astype(F32)[:, None, None]
        media_float = media_tokens.astype(F32)
        device = lax.axis_index("img") * lax.axis_size("lat") + lax.axis_index("lat")
        lanes = norm_gain.shape[-1]
        kinds = norm_gain.shape[1]
        norms = jnp.concatenate(
            [norm_gain.reshape(-1, lanes), norm_shift.reshape(-1, lanes)], axis=0
        )
        spread = jnp.zeros((16, model_width), BF16)
        spread = lax.dynamic_update_slice(spread, norms, (0, device * lanes))
        layers = []
        for level in range(LAYERS):
            extra = spread if level == 0 else None
            key_value_w, output_w, query_w, sums = gather_attention(
                lay, key_value_weight[level], output_weight[level], query_weight[level], extra
            )
            if level == 0:
                gain_all = sums[: LAYERS * kinds].reshape(LAYERS, kinds, model_width)
                shift_all = sums[LAYERS * kinds : 2 * LAYERS * kinds]
                shift_all = shift_all.reshape(LAYERS, kinds, model_width)
            up_w, down_w = gather_feed(lay, up_weight[level], down_weight[level])
            layers.append(
                (query_w, key_value_w, output_w, up_w, down_w, gain_all[level], shift_all[level])
            )
        latent_rows = jnp.broadcast_to(
            latent_init.astype(F32), (slot_count, latent_count, model_width)
        )
        stored_layers = []
        for level in range(LAYERS):
            latent_rows, stored = layer_forward(lay, latent_rows, media_float, layers[level])
            stored_layers.append(stored)
        resampled = latent_rows * valid_mask
        upstream = cotangent.astype(F32) * valid_mask
        media_grad = None
        attention = [None] * LAYERS
        feed = [None] * LAYERS
        terms = [None] * LAYERS
        for level in reversed(range(LAYERS)):
            upstream, d_media, attention[level], feed[level], terms[level] = layer_backward(
                lay, upstream, media_float, layers[level], stored_layers[level]
            )
            media_grad = d_media if media_grad is None else media_grad + d_media
        gains = [row for level in range(LAYERS) for row in terms[level][0]]
        shifts = [row for level in range(LAYERS) for row in terms[level][1]]
        small = jnp.stack(gains + shifts)
        pad = (-small.shape[0]) % 8
        small = jnp.pad(small, ((0, pad), (0, 0)))
        tail = jnp.concatenate([jnp.sum(upstream, axis=0), small], axis=0)
        tail = all_sum(tail, lay.img)
        latent_grad = tail[:latent_count]
        small = all_sum(tail[latent_count:], lay.lat)
        small = lax.dynamic_slice(small, (0, device * lanes), (2 * LAYERS * kinds, lanes))
        small = small.reshape(2, LAYERS, kinds, lanes)
        return (
            resampled,
            media_grad,
            latent_grad,
            jnp.stack([entry[2] for entry in attention]),
            jnp.stack([entry[0] for entry in attention]),
            jnp.stack([entry[1] for entry in attention]),
            jnp.stack([entry[0] for entry in feed]),
            jnp.stack([entry[1] for entry in feed]),
            small[0],
            small[1],
        )

    return per_device


def solution(mesh):
    lay = Layout(mesh.shape["img"], mesh.shape["lat"])
    in_specs = (
        P("img", "lat", None),
        P("img"),
        P("lat", None),
        P("img", "lat", None),
        P(None, ("img", "lat"), None),
        P(None, ("img", "lat"), None),
        P(None, ("img", "lat"), None),
        P(None, ("img", "lat"), None),
        P(None, ("img", "lat"), None),
        P(None, None, ("img", "lat")),
        P(None, None, ("img", "lat")),
    )
    out_specs = (
        P("img", "lat", None),
        P("img", "lat", None),
        P("lat", None),
        P(None, ("img", "lat"), None),
        P(None, ("img", "lat"), None),
        P(None, ("img", "lat"), None),
        P(None, ("img", "lat"), None),
        P(None, ("img", "lat"), None),
        P(None, None, ("img", "lat")),
        P(None, None, ("img", "lat")),
    )
    return jax.shard_map(
        make_device(lay), mesh=mesh, in_specs=in_specs, out_specs=out_specs, check_vma=False
    )
```

```python
import jax
import jax.numpy as jnp
from jax import lax
from jax.experimental import pallas as pl
from jax.experimental.pallas import tpu as pltpu
from jax.sharding import PartitionSpec as P

HEAD = 64
MEDIA = 5
LAYERS = 2
F32 = jnp.float32
BF16 = jnp.bfloat16
NORM_ROWS = 16


class Order:
    def __init__(self, token):
        self.token = token

    def gate(self, *arrays):
        arrays = lax.optimization_barrier(arrays + (self.token,))
        self.token = arrays[-1]
        return arrays[:-1] if len(arrays) > 2 else arrays[0]

    def all(self, arrays):
        arrays = lax.optimization_barrier(tuple(arrays) + (self.token,))
        self.token = arrays[-1]
        return list(arrays[:-1])

    def send(self, swap, array):
        return swap(self.gate(array))


class Bit:
    def __init__(self, axis, size, place, rank):
        self.rank = rank
        self.axis = axis
        self.mask = 1 << place
        self.pairs = [(source, source ^ self.mask) for source in range(size)]

    def mine(self):
        return (lax.axis_index(self.axis) // self.mask) % 2

    def swap(self, array):
        return lax.ppermute(array, self.axis, self.pairs)


class Four:
    def __init__(self, size, place):
        self.shift = 1 << place
        self.swaps = [self._swap(size, mask) for mask in (1, 2, 3)]

    def _swap(self, size, mask):
        pairs = [(source, source ^ (mask * self.shift)) for source in range(size)]
        return lambda array: lax.ppermute(array, "img", pairs)

    def mine(self):
        return (lax.axis_index("img") // self.shift) % 4

    def spread(self, order, array):
        return [order.send(swap, array) for swap in self.swaps]

    def merge(self, own, others, axis):
        pieces = [own] + others
        low = self.mine() % 2 == 0
        high = self.mine() // 2 == 0
        mixed = [
            [jnp.where(low, pieces[2 * a + b], pieces[2 * a + 1 - b]) for b in range(2)]
            for a in range(2)
        ]
        return jnp.stack(
            [jnp.where(high, mixed[c][b], mixed[1 - c][b]) for c in range(2) for b in range(2)],
            axis=axis,
        )

    def shed(self, order, terms, axis):
        me = self.mine()
        terms = list(order.all(terms))
        others = []
        for mask, swap in zip((1, 2, 3), self.swaps):
            sent = total([pick(term, me ^ mask, axis) for term in terms]).astype(BF16)
            others.append(order.send(swap, sent))
        return [pick(term, me, axis) for term in terms] + others


class Layout:
    def __init__(self, img, lat):
        lat_bits = [Bit("lat", lat, k, k) for k in range(lat.bit_length() - 1)]
        img_bits = [Bit("img", img, k, k + len(lat_bits)) for k in range(img.bit_length() - 1)]
        self.devices = img * lat
        self.lat = lat_bits[0]
        self.img = img_bits
        self.every = list(reversed(lat_bits + img_bits))
        self.first, self.second = img_bits[0], img_bits[1]
        self.far = list(reversed(img_bits[3:]))
        self.beyond = list(reversed(img_bits[4:]))
        self.plane = Four(img, 0)
        self.column = Four(img, 2)
        self.tensor = [img_bits[2], lat_bits[0]]
        self.split = 4
        self.outer = img // 16


def pick(array, index, axis):
    return lax.dynamic_index_in_dim(array, index, axis, keepdims=False)


def part(array, bit, place, own):
    return pick(array, bit.mine() if own else 1 - bit.mine(), place)


def pair(bit, own, other, axis):
    low = bit.mine() == 0
    return jnp.stack([jnp.where(low, own, other), jnp.where(low, other, own)], axis=axis)


def join(order, array, bits, have):
    have = list(have)
    for bit in bits:
        other = order.send(bit.swap, array)
        place = sum(1 for held in have if held.rank > bit.rank)
        array = pair(bit, array, other, place)
        have.insert(place, bit)
    return array, have


def total(terms):
    value = terms[0].astype(F32)
    for term in terms[1:]:
        value = value + term.astype(F32)
    return value


def shed(order, terms, bit, have):
    place = have.index(bit)
    terms = order.all(terms)
    sent = total([part(term, bit, place, False) for term in terms]).astype(BF16)
    other = order.send(bit.swap, sent)
    terms = [part(term, bit, place, True) for term in terms] + [other]
    return terms, [held for held in have if held is not bit]


def exchange(order, array, bit, place):
    other = order.send(bit.swap, part(array, bit, place, False))
    return pair(bit, part(array, bit, place, True), other, place)


def mm(a, b):
    return lax.dot_general(a, b, (((1,), (0,)), ((), ())), preferred_element_type=F32)


def mm_nt(a, b):
    return lax.dot_general(a, b, (((1,), (1,)), ((), ())), preferred_element_type=F32)


def mm_tn(a, b):
    return lax.dot_general(a, b, (((0,), (0,)), ((), ())), preferred_element_type=F32)


class Attention:
    def __init__(self, lay, order, kv_shard, out_shard, query_shard, extra):
        self.lay, self.order = lay, order
        self.rows, self.width = kv_shard.shape
        self.out_rows = out_shard.shape[0]
        half = self.width // 2
        outs = jnp.concatenate([out_shard[:, :half], out_shard[:, half:]], axis=0)
        parts = [kv_shard, jnp.concatenate([query_shard, outs], axis=1)]
        if extra is not None:
            parts.append(extra)
        self.extra = extra is not None
        self.own = jnp.concatenate(parts, axis=0)

    def start_column(self):
        lay = self.lay
        self.own, _ = join(self.order, self.own, lay.beyond, [])
        self.own = self.own.reshape((lay.outer,) + self.own.shape[-2:])
        self.others = lay.column.spread(self.order, self.own)

    def end_column(self):
        own, *others = self.order.all([self.own] + self.others)
        self.own = self.lay.column.merge(own, others, 1)

    def start_plane(self):
        self.others = self.lay.plane.spread(self.order, self.own)

    def end_plane(self):
        own, *others = self.order.all([self.own] + self.others)
        self.own = self.lay.plane.merge(own, others, 2)

    def start_lat(self):
        self.others = self.order.send(self.lay.lat.swap, self.own)

    def end_lat(self):
        lay, rows, width = self.lay, self.rows, self.width
        half = width // 2
        self.own, self.others = self.order.gate(self.own, self.others)

        def both(select):
            return pair(lay.lat, select(self.own), select(self.others), 3)

        key_value = both(lambda a: a[..., :rows, :]).reshape(-1, width)
        query = both(lambda a: a[..., rows : 2 * rows, :half]).reshape(-1, half)
        middle = rows + self.out_rows
        output = both(
            lambda a: jnp.concatenate(
                [a[..., rows:middle, half:], a[..., middle : 2 * rows, half:]], axis=-1
            )
        ).reshape(-1, width)
        if self.extra:
            own = self.own[..., 2 * rows :, :].astype(F32)
            other = self.others[..., 2 * rows :, :].astype(F32)
            self.norms = jnp.sum(own, axis=(0, 1, 2)) + jnp.sum(other, axis=(0, 1, 2))
        return query, key_value, output


def feed_columns(lay, array, forward):
    width = array.shape[-1] // lay.devices if forward else None
    ranks = [bit.rank for bit in lay.tensor]
    owner = []
    for device in range(lay.devices):
        value = 0
        for rank in ranks:
            value = value * 2 + (device >> rank) % 2
        owner.append(value)
    if forward:
        blocks = [array[..., d * width : (d + 1) * width] for d in range(lay.devices)]
        sets = [
            jnp.concatenate([blocks[d] for d in range(lay.devices) if owner[d] == s], axis=-1)
            for s in range(lay.split)
        ]
        return jnp.stack(sets)
    width = array.shape[-1] * lay.split // lay.devices
    seen = [0] * lay.split
    blocks = []
    for device in range(lay.devices):
        s = owner[device]
        blocks.append(array[s, :, seen[s] * width : (seen[s] + 1) * width])
        seen[s] += 1
    return jnp.concatenate(blocks, axis=-1)


class Feed:
    def __init__(self, lay, order, up_shard, down_shard):
        self.lay, self.order = lay, order
        self.rows = up_shard.shape[0]
        self.columns = up_shard.shape[1] // lay.split
        up = feed_columns(lay, up_shard, True)
        self.up = up.reshape((2, 2, self.rows, self.columns))
        self.down = down_shard

    def start_lat(self):
        self.other = self.order.send(self.lay.lat.swap, part(self.up, self.lay.lat, 1, False))

    def start_near(self):
        self.up, self.other = self.order.gate(self.up, self.other)
        own = part(self.up, self.lay.lat, 1, True)
        self.up = pair(self.lay.lat, own, self.other, 1)
        near = self.lay.tensor[0]
        self.other = self.order.send(near.swap, part(self.up, near, 0, False))

    def start_far(self):
        near = self.lay.tensor[0]
        self.up, self.other = self.order.gate(self.up, self.other)
        up = pair(near, part(self.up, near, 0, True), self.other, 0)
        packed = jnp.concatenate([up.reshape(-1, self.columns), self.down], axis=0)
        packed, self.have = join(self.order, packed, self.lay.far[:-1], [])
        self.own = packed
        self.other = self.order.send(self.lay.far[-1].swap, packed)

    def end_far(self):
        place = len(self.have)
        self.own, self.other = self.order.gate(self.own, self.other)
        packed = pair(self.lay.far[-1], self.own, self.other, place)
        self.have = self.have + [self.lay.far[-1]]
        cut = self.rows * self.lay.split
        up = packed[..., :cut, :]
        self.up = up.reshape((2,) * (len(self.have) + 2) + (self.rows, self.columns))
        self.down = packed[..., cut:, :]

    def start_plane(self):
        lay = self.lay
        self.up_other = self.order.send(lay.first.swap, self.up)
        self.down_other = self.order.send(lay.second.swap, self.down)

    def gate(self):
        arrays = [self.up, self.up_other, self.down, self.down_other]
        self.up, self.up_other, self.down, self.down_other = self.order.all(arrays)

    def next_plane(self):
        lay = self.lay
        place = len(self.have)
        self.gate()
        self.up = pair(lay.first, self.up, self.up_other, place + 1)
        self.down = pair(lay.second, self.down, self.down_other, place)
        self.up_other = self.order.send(lay.second.swap, self.up)
        self.down_other = self.order.send(lay.first.swap, self.down)

    def end_plane(self):
        lay = self.lay
        place = len(self.have)
        self.gate()
        up = pair(lay.second, self.up, self.up_other, place + 1)
        down = pair(lay.first, self.down, self.down_other, place + 1)
        return up.reshape(-1, self.columns), down.reshape(-1, self.columns)


class FeedGrad:
    def __init__(self, lay, order, up_term, down_term, rows):
        self.lay, self.order, self.rows = lay, order, rows
        self.columns = up_term.shape[1]
        self.up_have = lay.every
        self.up = [up_term.reshape((2,) * len(lay.every) + (rows, self.columns))]
        self.down_have = [bit for bit in lay.every if bit not in lay.tensor]
        self.down = [down_term.reshape((2,) * len(self.down_have) + (-1, self.columns))]

    def plane(self, turn):
        lay = self.lay
        bits = (lay.second, lay.first) if turn == 0 else (lay.first, lay.second)
        self.up, self.up_have = shed(self.order, self.up, bits[0], self.up_have)
        self.down, self.down_have = shed(self.order, self.down, bits[1], self.down_have)

    def far(self):
        lay = self.lay
        lead = (2,) * len(lay.far)
        count = len(self.up)
        both = self.order.all(self.up + self.down)
        self.up, self.down = both[:count], both[count:]
        terms = []
        for up, down in zip(self.up, self.down):
            up = up.reshape(lead + (-1, self.columns))
            terms.append(jnp.concatenate([up, down], axis=-2))
        have = list(lay.far)
        for bit in reversed(lay.far):
            terms, have = shed(self.order, terms, bit, have)
        self.terms = terms

    def start_near(self):
        cut = self.rows * self.lay.split
        packed = total(self.order.all(self.terms))
        self.down = packed[cut:]
        self.up = packed[:cut].astype(BF16).reshape(2, 2, self.rows, self.columns)
        near = self.lay.tensor[0]
        self.other = self.order.send(near.swap, part(self.up, near, 0, False))

    def start_lat(self):
        near, lat = self.lay.tensor
        self.up, self.other = self.order.gate(self.up, self.other)
        self.up = pair(near, part(self.up, near, 0, True), self.other, 0)
        self.other = self.order.send(lat.swap, part(self.up, lat, 1, False))

    def end(self):
        lat = self.lay.lat
        self.up, self.other = self.order.gate(self.up, self.other)
        up = pair(lat, part(self.up, lat, 1, True), self.other, 1)
        up = feed_columns(self.lay, up.reshape(self.lay.split, self.rows, self.columns), False)
        return up.astype(F32), self.down


class AttentionGrad:
    def __init__(self, lay, order, term):
        self.lay, self.order = lay, order
        self.terms = [term.reshape((lay.outer, 4, 4, 2) + term.shape[1:])]

    def lat(self):
        have = [None, None, None, self.lay.lat]
        self.terms, _ = shed(self.order, self.terms, self.lay.lat, have)

    def plane(self):
        self.terms = self.lay.plane.shed(self.order, self.terms, 2)

    def column(self):
        self.terms = self.lay.column.shed(self.order, self.terms, 1)

    def end(self):
        lay = self.lay
        terms = [t.reshape((2,) * len(lay.beyond) + t.shape[1:]) for t in self.terms]
        have = list(lay.beyond)
        for bit in reversed(lay.beyond):
            terms, have = shed(self.order, terms, bit, have)
        return total(terms)


def normalize(rows):
    centered = rows - jnp.mean(rows, axis=-1, keepdims=True)
    rate = lax.rsqrt(jnp.mean(centered * centered, axis=-1, keepdims=True) + 1e-05)
    return centered * rate, rate


def norm_back(grad, rows, gain):
    unit, rate = normalize(rows)
    scaled = grad * gain
    mean = jnp.mean(scaled, axis=-1, keepdims=True)
    along = jnp.mean(scaled * unit, axis=-1, keepdims=True)
    return rate * (scaled - mean - unit * along), jnp.sum(grad * unit, axis=0), jnp.sum(grad, axis=0)


def head_mask(rows, heads, width):
    row = lax.broadcasted_iota(jnp.int32, (heads * rows, width), 0) // rows
    column = lax.broadcasted_iota(jnp.int32, (heads * rows, width), 1) // (width // heads)
    return row == column


def spread_heads(rows, mask, heads):
    return jnp.where(mask, jnp.concatenate([rows] * heads, axis=0), 0)


def merge_heads(array, mask, heads):
    kept = jnp.where(mask, array, 0)
    size = array.shape[0] // heads
    total = kept[:size]
    for head in range(1, heads):
        total = total + kept[head * size : (head + 1) * size]
    return total


def slot_pairs(refs, slot, slots):
    return jnp.concatenate(
        [ref[slot * (ref.shape[0] // slots) : (slot + 1) * (ref.shape[0] // slots)] for ref in refs],
        axis=0,
    )


def soft_scores(query_wide, keys):
    scores = mm_nt(query_wide, keys)
    exponent = jnp.exp(scores - jnp.max(scores, axis=-1, keepdims=True))
    return exponent / jnp.sum(exponent, axis=-1, keepdims=True)


def attend_kernel(slots, heads, spot, refs):
    query, own_m, other_m, own_l, other_l, rows, output_w, norms, mixed, after, normed = refs
    width = query.shape[1]
    count = query.shape[0] // slots
    mask = head_mask(count, heads, width)
    for slot in range(slots):
        pairs = slot_pairs((own_m, other_m, own_l, other_l), slot, slots)
        place = slice(slot * count, (slot + 1) * count)
        wide = spread_heads(query[place] * 0.125, mask, heads)
        probs = soft_scores(wide, pairs[:, :width]).astype(BF16)
        mixed[place] = merge_heads(mm(probs, pairs[:, width:]), mask, heads).astype(BF16)
    total = rows[...] + mm(mixed[...], output_w[...])
    after[...] = total
    unit, _ = normalize(total)
    normed[...] = (unit * norms[spot[0] : spot[0] + 1] + norms[spot[1] : spot[1] + 1]).astype(BF16)


def near_memory(arrays):
    return list(arrays)


def attend(slots, heads, spot, query, own_m, other_m, own_l, other_l, rows, output_w, norms):
    shape = jax.ShapeDtypeStruct
    return pl.pallas_call(
        lambda *refs: attend_kernel(slots, heads, spot, refs),
        out_shape=(
            shape(query.shape, BF16),
            shape(rows.shape, F32),
            shape(rows.shape, BF16),
        ),
        in_specs=[pl.BlockSpec(memory_space=pltpu.VMEM)] * 8,
        out_specs=(pl.BlockSpec(memory_space=pltpu.VMEM),) * 3,
        cost_estimate=pl.CostEstimate(flops=4000000000, bytes_accessed=6000000, transcendentals=410000),
        name="attend",
    )(*near_memory((query, own_m, other_m, own_l, other_l, rows, output_w, norms)))


def attend_back_kernel(slots, heads, spot, refs):
    (
        normed_grad,
        upstream,
        after,
        query,
        own_m,
        other_m,
        own_l,
        other_l,
        mixed,
        output_w,
        norms,
        d_after,
        d_query,
        d_own_m,
        d_other_m,
        d_own_l,
        d_other_l,
        output_grad,
        norm_grad,
    ) = refs
    width = query.shape[1]
    count = query.shape[0] // slots
    mask = head_mask(count, heads, width)
    grad, d_gain, d_shift = norm_back(normed_grad[...], after[...], norms[spot : spot + 1])
    grad = grad + upstream[...]
    d_after[...] = grad
    norm_grad[...] = jnp.zeros_like(norm_grad)
    norm_grad[0:1] = d_gain[None]
    norm_grad[1:2] = d_shift[None]
    low = grad.astype(BF16)
    output_grad[...] = mm_tn(mixed[...], low).astype(BF16)
    mixed_grad = mm_nt(low, output_w[...]).astype(BF16)
    outs = (d_own_m, d_other_m, d_own_l, d_other_l)
    for slot in range(slots):
        pairs = slot_pairs((own_m, other_m, own_l, other_l), slot, slots)
        keys, values = pairs[:, :width], pairs[:, width:]
        place = slice(slot * count, (slot + 1) * count)
        wide = spread_heads(query[place] * 0.125, mask, heads)
        soft = soft_scores(wide, keys)
        wide_grad = spread_heads(mixed_grad[place], mask, heads)
        d_probs = mm_nt(wide_grad, values)
        d_values = mm_tn(soft.astype(BF16), wide_grad).astype(BF16)
        d_scores = soft * (d_probs - jnp.sum(d_probs * soft, axis=-1, keepdims=True))
        d_scores = d_scores.astype(BF16)
        d_keys = mm_tn(d_scores, wide).astype(BF16)
        d_query[place] = (merge_heads(mm(d_scores, keys), mask, heads) * 0.125).astype(BF16)
        start = 0
        for ref in outs:
            size = ref.shape[0] // slots
            ref[slot * size : (slot + 1) * size, :width] = d_keys[start : start + size]
            ref[slot * size : (slot + 1) * size, width:] = d_values[start : start + size]
            start += size


def attend_back(
    slots, heads, spot, normed_grad, upstream, after, query, pairs, mixed, output_w, norms
):
    shape = jax.ShapeDtypeStruct
    own_m, other_m, own_l, other_l = pairs
    return pl.pallas_call(
        lambda *refs: attend_back_kernel(slots, heads, spot, refs),
        out_shape=(
            shape(after.shape, F32),
            shape(query.shape, BF16),
            shape(own_m.shape, BF16),
            shape(other_m.shape, BF16),
            shape(own_l.shape, BF16),
            shape(other_l.shape, BF16),
            shape(output_w.shape, BF16),
            shape((8, after.shape[1]), F32),
        ),
        in_specs=[pl.BlockSpec(memory_space=pltpu.VMEM)] * 11,
        out_specs=(pl.BlockSpec(memory_space=pltpu.VMEM),) * 8,
        cost_estimate=pl.CostEstimate(flops=8000000000, bytes_accessed=12000000, transcendentals=410000),
        name="attend_back",
    )(
        *near_memory(
            (normed_grad, upstream, after, query)
            + (own_m, other_m, own_l, other_l, mixed, output_w, norms)
        )
    )


class Step:
    def __init__(self, lay, order, slots, media_rows, norms, level):
        self.lay, self.order, self.slots = lay, order, slots
        self.media_rows = media_rows
        self.norms = norms
        kinds = 3
        self.gains = [norms[level * kinds + k][None] for k in range(kinds)]
        self.shifts = [norms[(LAYERS + level) * kinds + k][None] for k in range(kinds)]
        self.spots = (level * kinds + 2, (LAYERS + level) * kinds + 2)

    def media(self, query_w, key_value_w, output_w):
        self.query_w, self.key_value_w, self.output_w = query_w, key_value_w, output_w
        self.heads = query_w.shape[1] // HEAD
        unit, _ = normalize(self.media_rows.astype(F32))
        self.media_norm = (unit * self.gains[0] + self.shifts[0]).astype(BF16)
        self.own_m = mm(self.media_norm, key_value_w).astype(BF16)
        self.other_m = self.order.send(self.lay.lat.swap, self.own_m)

    def latents(self, rows):
        self.rows = rows
        unit, _ = normalize(rows)
        self.latent_norm = (unit * self.gains[1] + self.shifts[1]).astype(BF16)
        self.own_l = mm(self.latent_norm, self.key_value_w).astype(BF16)
        self.other_l = self.order.send(self.lay.lat.swap, self.own_l)
        self.query = mm(self.latent_norm, self.query_w).astype(BF16)

    def attention(self):
        query, self.other_m, self.other_l = self.order.gate(self.query, self.other_m, self.other_l)
        self.mixed, self.after, self.normed = attend(
            self.slots,
            self.heads,
            self.spots,
            query,
            self.own_m,
            self.other_m,
            self.own_l,
            self.other_l,
            self.rows,
            self.output_w,
            self.norms,
        )

    def feed(self, shared, up_w, down_w):
        self.shared, self.up_w, self.down_w = shared, up_w, down_w
        shared = self.order.gate(shared)
        hidden = mm(shared, up_w)
        big = 0.5 * (1.0 + lax.erf(hidden * (2.0**-0.5)))
        density = jnp.exp(-0.5 * hidden * hidden) * ((2.0 * jnp.pi) ** -0.5)
        self.active = (hidden * big).astype(BF16)
        self.slope = (big + hidden * density).astype(BF16)
        return mm(self.active, down_w).astype(BF16)

    def feed_back(self, branch):
        branch = self.order.gate(branch)
        self.branch = branch
        self.d_hidden = (mm_nt(branch, self.down_w) * self.slope.astype(F32)).astype(BF16)
        return mm_nt(self.d_hidden, self.up_w).astype(BF16)

    def feed_terms(self):
        down = mm_tn(self.active, self.order.gate(self.branch)).astype(BF16)
        up = mm_tn(self.shared, self.d_hidden).astype(BF16)
        rows = up.shape[0] // self.lay.devices
        return FeedGrad(self.lay, self.order, up, down, rows)

    def attention_back(self, normed_grad, upstream):
        normed_grad = self.order.gate(normed_grad)
        (
            self.d_after,
            self.d_query,
            self.d_own_m,
            d_other_m,
            self.d_own_l,
            d_other_l,
            self.output_term,
            self.feed_norm,
        ) = attend_back(
            self.slots,
            self.heads,
            self.spots[0],
            normed_grad,
            upstream,
            self.after,
            self.query,
            (self.own_m, self.other_m, self.own_l, self.other_l),
            self.mixed,
            self.output_w,
            self.norms,
        )
        self.back_l = self.order.send(self.lay.lat.swap, d_other_l)
        self.back_m = self.order.send(self.lay.lat.swap, d_other_m)

    def latents_back(self):
        pairs_l = total(self.order.gate(self.d_own_l, self.back_l)).astype(BF16)
        self.pairs_l = pairs_l
        d_norm = mm_nt(pairs_l, self.key_value_w) + mm_nt(self.d_query, self.query_w)
        d_rows, self.gain_l, self.shift_l = norm_back(d_norm, self.rows, self.gains[1])
        return d_rows + self.d_after

    def right_term(self):
        lay = self.lay
        latent_norm = self.order.gate(self.latent_norm)
        width = self.output_w.shape[1]
        half = width // 2
        query = mm_tn(latent_norm, self.d_query).astype(BF16)
        query = query.reshape(lay.devices, -1, half)
        output = self.output_term.reshape(lay.devices, -1, width)
        output = jnp.concatenate([output[..., :half], output[..., half:]], axis=1)
        return AttentionGrad(lay, self.order, jnp.concatenate([query, output], axis=-1))

    def left_term(self):
        lay = self.lay
        pairs_m = total(self.order.gate(self.d_own_m, self.back_m)).astype(BF16)
        self.pairs_m = pairs_m
        term = (mm_tn(self.media_norm, pairs_m) + mm_tn(self.latent_norm, self.pairs_l)).astype(BF16)
        return AttentionGrad(lay, self.order, term.reshape(lay.devices, -1, term.shape[1]))

    def media_back(self):
        pairs_m = self.order.gate(self.pairs_m)
        d_norm = mm_nt(pairs_m, self.key_value_w)
        rows = self.media_rows.astype(F32)
        d_media, self.gain_m, self.shift_m = norm_back(d_norm, rows, self.gains[0])
        return d_media

    def norm_terms(self):
        gains = [self.gain_m, self.gain_l, self.feed_norm[0]]
        shifts = [self.shift_m, self.shift_l, self.feed_norm[1]]
        return gains, shifts


def gather_near(lay, order, rows):
    return rows, order.send(lay.tensor[0].swap, rows)


def gather_lat(lay, order, pieces):
    rows = jnp.concatenate(order.all(pieces), axis=0)
    return rows, order.send(lay.lat.swap, rows)


def return_lat(lay, order, rows):
    half = rows.shape[0] // 2
    return rows[:half], order.send(lay.lat.swap, rows[half:])


def return_near(lay, order, terms):
    half = terms[0].shape[0] // 2
    terms = order.all(terms)
    sent = total([term[half:] for term in terms]).astype(BF16)
    return [term[:half] for term in terms] + [order.send(lay.tensor[0].swap, sent)]


def make_device(lay):
    def per_device(
        media_tokens,
        image_counts,
        latent_init,
        cotangent,
        query_weight,
        key_value_weight,
        output_weight,
        up_weight,
        down_weight,
        norm_gain,
        norm_shift,
    ):
        first = norm_gain[0, :1].astype(F32)
        order = Order(first)
        slots = media_tokens.shape[0]
        model = media_tokens.shape[2]
        count = latent_init.shape[0]
        position = jnp.arange(slots) % MEDIA
        per_slot = jnp.repeat(image_counts, MEDIA)
        valid = (position < per_slot).astype(F32)[:, None, None]
        row_mask = jnp.broadcast_to(valid, (slots, count, 1)).reshape(-1, 1)
        media_rows = media_tokens.reshape(-1, model)
        device = lax.axis_index("img") * lax.axis_size("lat") + lax.axis_index("lat")
        lanes = norm_gain.shape[-1]
        kinds = norm_gain.shape[1]
        norms = jnp.concatenate(
            [norm_gain.reshape(-1, lanes), norm_shift.reshape(-1, lanes)], axis=0
        )
        spread = jnp.zeros((NORM_ROWS, model), BF16)
        spread = lax.dynamic_update_slice(spread, norms, (0, device * lanes))
        attn = [
            Attention(
                lay,
                order,
                key_value_weight[level],
                output_weight[level],
                query_weight[level],
                spread if level == 0 else None,
            )
            for level in range(LAYERS)
        ]
        feed = [Feed(lay, order, up_weight[level], down_weight[level]) for level in range(LAYERS)]
        upstream = cotangent.astype(F32).reshape(-1, model) * row_mask

        attn[0].start_column()
        feed[0].start_lat()
        feed[1].start_lat()
        feed[0].start_near()
        feed[1].start_near()
        attn[0].end_column()
        attn[0].start_plane()
        feed[0].start_far()
        attn[0].end_plane()
        attn[0].start_lat()
        feed[0].end_far()
        feed[0].start_plane()
        weights = attn[0].end_lat()
        step0 = Step(lay, order, slots, media_rows, attn[0].norms, 0)
        step0.media(*weights)
        rows0 = jnp.broadcast_to(latent_init.astype(F32), (slots, count, model)).reshape(-1, model)
        step0.latents(rows0)
        attn[1].start_column()
        feed[0].next_plane()
        attn[1].end_column()
        feed[1].start_far()
        step0.attention()
        pieces = gather_near(lay, order, step0.normed)
        pieces = gather_lat(lay, order, pieces)
        feed_w = feed[0].end_plane()
        attn[1].start_plane()
        out = step0.feed(jnp.concatenate(order.all(pieces), axis=0), *feed_w)
        terms = return_lat(lay, order, out)
        feed[1].end_far()
        terms = return_near(lay, order, terms)
        attn[1].end_plane()
        attn[1].start_lat()
        feed[1].start_plane()
        rows1 = step0.after + total(order.all(terms))
        weights = attn[1].end_lat()
        step1 = Step(lay, order, slots, media_rows, attn[0].norms, 1)
        step1.media(*weights)
        step1.latents(rows1)
        feed[1].next_plane()
        branch = gather_near(lay, order, upstream.astype(BF16))
        step1.attention()
        pieces = gather_near(lay, order, step1.normed)
        branch = gather_lat(lay, order, branch)
        pieces = gather_lat(lay, order, pieces)
        feed_w = feed[1].end_plane()
        out = step1.feed(jnp.concatenate(order.all(pieces), axis=0), *feed_w)
        terms_out = return_lat(lay, order, out)
        out = step1.feed_back(jnp.concatenate(order.all(branch), axis=0))
        terms = return_lat(lay, order, out)
        feed_grad1 = step1.feed_terms()
        terms = return_near(lay, order, terms)
        feed_grad1.plane(0)
        terms_out = return_near(lay, order, terms_out)
        step1.attention_back(total(order.all(terms)), upstream)
        upstream0 = step1.latents_back()
        branch = gather_near(lay, order, upstream0.astype(BF16))
        right1 = step1.right_term()
        right1.lat()
        left1 = step1.left_term()
        left1.lat()
        branch = gather_lat(lay, order, branch)
        feed_grad1.plane(1)
        out = step0.feed_back(jnp.concatenate(order.all(branch), axis=0))
        terms = return_lat(lay, order, out)
        feed_grad0 = step0.feed_terms()
        terms = return_near(lay, order, terms)
        feed_grad1.far()
        right1.plane()
        left1.plane()
        media1 = step1.media_back()
        step0.attention_back(total(order.all(terms)), upstream0)
        feed_grad1.start_near()
        feed_grad0.plane(0)
        last = step0.latents_back()
        right0 = step0.right_term()
        right0.lat()
        left0 = step0.left_term()
        left0.lat()
        right1.column()
        left1.column()
        feed_grad1.start_lat()
        feed_grad0.plane(1)
        right0.plane()
        left0.plane()
        media_grad = media1 + step0.media_back()
        gains0, shifts0 = step0.norm_terms()
        gains1, shifts1 = step1.norm_terms()
        small = jnp.stack(gains0 + gains1 + shifts0 + shifts1)
        small = jnp.pad(small, ((0, NORM_ROWS - small.shape[0]), (0, 0)))
        latent = jnp.sum(last.reshape(slots, count, model), axis=0)
        tail = jnp.concatenate([latent, small], axis=0)
        for bit in lay.img[:2]:
            tail = tail + order.send(bit.swap, tail)
        feed_grad0.far()
        right0.column()
        left0.column()
        for bit in lay.img[2:]:
            tail = tail + order.send(bit.swap, tail)
        feed_grad0.start_near()
        feed_grad0.start_lat()
        small = tail[count:]
        small = small + order.send(lay.lat.swap, small)
        small = lax.dynamic_slice(small, (0, device * lanes), (2 * LAYERS * kinds, lanes))
        small = small + (order.token - first)
        small = small.reshape(2, LAYERS, kinds, lanes)
        rights = [right0.end(), right1.end()]
        lefts = [left0.end(), left1.end()]
        feeds = [feed_grad0.end(), feed_grad1.end()]
        half = model // 2
        outs = []
        for right in rights:
            cut = right.shape[0] // 2
            outs.append(jnp.concatenate([right[:cut, half:], right[cut:, half:]], axis=1))
        resampled = ((step1.after + total(terms_out)) * row_mask).reshape(cotangent.shape)
        return (
            resampled,
            media_grad.reshape(media_tokens.shape),
            tail[:count],
            jnp.stack([right[:, :half] for right in rights]),
            jnp.stack(lefts),
            jnp.stack(outs),
            jnp.stack([entry[0] for entry in feeds]),
            jnp.stack([entry[1] for entry in feeds]),
            small[0],
            small[1],
        )

    return per_device


def solution(mesh):
    lay = Layout(mesh.shape["img"], mesh.shape["lat"])
    in_specs = (
        P("img", "lat", None),
        P("img"),
        P("lat", None),
        P("img", "lat", None),
        P(None, ("img", "lat"), None),
        P(None, ("img", "lat"), None),
        P(None, ("img", "lat"), None),
        P(None, ("img", "lat"), None),
        P(None, ("img", "lat"), None),
        P(None, None, ("img", "lat")),
        P(None, None, ("img", "lat")),
    )
    out_specs = (
        P("img", "lat", None),
        P("img", "lat", None),
        P("lat", None),
        P(None, ("img", "lat"), None),
        P(None, ("img", "lat"), None),
        P(None, ("img", "lat"), None),
        P(None, ("img", "lat"), None),
        P(None, ("img", "lat"), None),
        P(None, None, ("img", "lat")),
        P(None, None, ("img", "lat")),
    )
    return jax.shard_map(
        make_device(lay), mesh=mesh, in_specs=in_specs, out_specs=out_specs, check_vma=False
    )
```

```python
import jax
import jax.numpy as jnp
from jax import lax
from jax.experimental import pallas as pl
from jax.experimental.pallas import tpu as pltpu
from jax.sharding import PartitionSpec as P

HEAD = 64
MEDIA = 5
LAYERS = 2
F32 = jnp.float32
BF16 = jnp.bfloat16
NORM_ROWS = 16
LIGHT = pl.CostEstimate(flops=1, bytes_accessed=1, transcendentals=0)


class Order:
    def __init__(self, token):
        self.token = token

    def gate(self, *arrays):
        arrays = lax.optimization_barrier(arrays + (self.token,))
        self.token = arrays[-1]
        return arrays[:-1] if len(arrays) > 2 else arrays[0]

    def all(self, arrays):
        arrays = lax.optimization_barrier(tuple(arrays) + (self.token,))
        self.token = arrays[-1]
        return list(arrays[:-1])

    def send(self, swap, array):
        return swap(self.gate(array))


class Bit:
    def __init__(self, axis, size, place, rank):
        self.rank = rank
        self.axis = axis
        self.mask = 1 << place
        self.pairs = [(source, source ^ self.mask) for source in range(size)]

    def mine(self):
        return (lax.axis_index(self.axis) // self.mask) % 2

    def swap(self, array):
        return lax.ppermute(array, self.axis, self.pairs)


class Four:
    def __init__(self, size, place):
        self.shift = 1 << place
        self.swaps = [self._swap(size, mask) for mask in (1, 2, 3)]

    def _swap(self, size, mask):
        pairs = [(source, source ^ (mask * self.shift)) for source in range(size)]
        return lambda array: lax.ppermute(array, "img", pairs)

    def mine(self):
        return (lax.axis_index("img") // self.shift) % 4

    def spread(self, order, array):
        return [order.send(swap, array) for swap in self.swaps]

    def merge(self, own, others, axis):
        pieces = [own] + others
        low = self.mine() % 2 == 0
        high = self.mine() // 2 == 0
        mixed = [
            [jnp.where(low, pieces[2 * a + b], pieces[2 * a + 1 - b]) for b in range(2)]
            for a in range(2)
        ]
        return jnp.stack(
            [jnp.where(high, mixed[c][b], mixed[1 - c][b]) for c in range(2) for b in range(2)],
            axis=axis,
        )

    def add(self, order, array, others):
        array, *others = order.all([array] + others)
        return (array + others[0]) + (others[1] + others[2])

    def shed(self, order, terms, axis):
        me = self.mine()
        terms = list(order.all(terms))
        others = []
        for mask, swap in zip((1, 2, 3), self.swaps):
            sent = total([pick(term, me ^ mask, axis) for term in terms]).astype(BF16)
            others.append(order.send(swap, sent))
        return [pick(term, me, axis) for term in terms] + others


class Layout:
    def __init__(self, img, lat):
        lat_bits = [Bit("lat", lat, k, k) for k in range(lat.bit_length() - 1)]
        img_bits = [Bit("img", img, k, k + len(lat_bits)) for k in range(img.bit_length() - 1)]
        self.devices = img * lat
        self.lat = lat_bits[0]
        self.img = img_bits
        self.every = list(reversed(lat_bits + img_bits))
        self.first, self.second = img_bits[0], img_bits[1]
        self.far = list(reversed(img_bits[3:]))
        self.beyond = list(reversed(img_bits[4:]))
        self.plane = Four(img, 0)
        self.column = Four(img, 2)
        self.tensor = [img_bits[2], lat_bits[0]]
        self.split = 4
        self.outer = img // 16


def pick(array, index, axis):
    return lax.dynamic_index_in_dim(array, index, axis, keepdims=False)


def part(array, bit, place, own):
    return pick(array, bit.mine() if own else 1 - bit.mine(), place)


def pair(bit, own, other, axis):
    low = bit.mine() == 0
    return jnp.stack([jnp.where(low, own, other), jnp.where(low, other, own)], axis=axis)


def join(order, array, bits, have):
    have = list(have)
    for bit in bits:
        other = order.send(bit.swap, array)
        place = sum(1 for held in have if held.rank > bit.rank)
        array = pair(bit, array, other, place)
        have.insert(place, bit)
    return array, have


def total(terms):
    value = terms[0].astype(F32)
    for term in terms[1:]:
        value = value + term.astype(F32)
    return value


def shed(order, terms, bit, have):
    place = have.index(bit)
    terms = order.all(terms)
    sent = total([part(term, bit, place, False) for term in terms]).astype(BF16)
    other = order.send(bit.swap, sent)
    terms = [part(term, bit, place, True) for term in terms] + [other]
    return terms, [held for held in have if held is not bit]


def exchange(order, array, bit, place):
    other = order.send(bit.swap, part(array, bit, place, False))
    return pair(bit, part(array, bit, place, True), other, place)


def mm(a, b):
    return lax.dot_general(a, b, (((1,), (0,)), ((), ())), preferred_element_type=F32)


def mm_nt(a, b):
    return lax.dot_general(a, b, (((1,), (1,)), ((), ())), preferred_element_type=F32)


def mm_tn(a, b):
    return lax.dot_general(a, b, (((0,), (0,)), ((), ())), preferred_element_type=F32)


class Attention:
    def __init__(self, lay, order, kv_shard, out_shard, query_shard, extra):
        self.lay, self.order = lay, order
        self.rows, self.width = kv_shard.shape
        self.out_rows = out_shard.shape[0]
        half = self.width // 2
        outs = jnp.concatenate([out_shard[:, :half], out_shard[:, half:]], axis=0)
        parts = [kv_shard, jnp.concatenate([query_shard, outs], axis=1)]
        if extra is not None:
            parts.append(extra)
        self.extra = extra is not None
        self.own = jnp.concatenate(parts, axis=0)

    def start_column(self):
        lay = self.lay
        self.own, _ = join(self.order, self.own, lay.beyond, [])
        self.own = self.own.reshape((lay.outer,) + self.own.shape[-2:])
        self.others = lay.column.spread(self.order, self.own)

    def end_column(self):
        own, *others = self.order.all([self.own] + self.others)
        self.own = self.lay.column.merge(own, others, 1)

    def start_plane(self):
        self.others = self.lay.plane.spread(self.order, self.own)

    def end_plane(self):
        own, *others = self.order.all([self.own] + self.others)
        self.own = self.lay.plane.merge(own, others, 2)

    def start_lat(self):
        self.others = self.order.send(self.lay.lat.swap, self.own)

    def end_lat(self):
        lay, rows, width = self.lay, self.rows, self.width
        half = width // 2
        self.own, self.others = self.order.gate(self.own, self.others)

        def both(select):
            return pair(lay.lat, select(self.own), select(self.others), 3)

        key_value = both(lambda a: a[..., :rows, :]).reshape(-1, width)
        query = both(lambda a: a[..., rows : 2 * rows, :half]).reshape(-1, half)
        middle = rows + self.out_rows
        output = both(
            lambda a: jnp.concatenate(
                [a[..., rows:middle, half:], a[..., middle : 2 * rows, half:]], axis=-1
            )
        ).reshape(-1, width)
        if self.extra:
            own = self.own[..., 2 * rows :, :].astype(F32)
            other = self.others[..., 2 * rows :, :].astype(F32)
            self.norms = jnp.sum(own, axis=(0, 1, 2)) + jnp.sum(other, axis=(0, 1, 2))
        return query, key_value, output


def feed_columns(lay, array, forward):
    width = array.shape[-1] // lay.devices if forward else None
    ranks = [bit.rank for bit in lay.tensor]
    owner = []
    for device in range(lay.devices):
        value = 0
        for rank in ranks:
            value = value * 2 + (device >> rank) % 2
        owner.append(value)
    if forward:
        blocks = [array[..., d * width : (d + 1) * width] for d in range(lay.devices)]
        sets = [
            jnp.concatenate([blocks[d] for d in range(lay.devices) if owner[d] == s], axis=-1)
            for s in range(lay.split)
        ]
        return jnp.stack(sets)
    width = array.shape[-1] * lay.split // lay.devices
    seen = [0] * lay.split
    blocks = []
    for device in range(lay.devices):
        s = owner[device]
        blocks.append(array[s, :, seen[s] * width : (seen[s] + 1) * width])
        seen[s] += 1
    return jnp.concatenate(blocks, axis=-1)


class Feed:
    def __init__(self, lay, order, up_shard, down_shard):
        self.lay, self.order = lay, order
        self.rows = up_shard.shape[0]
        self.columns = up_shard.shape[1] // lay.split
        up = feed_columns(lay, up_shard, True)
        self.up = up.reshape((2, 2, self.rows, self.columns))
        self.down = down_shard

    def start_lat(self):
        self.other = self.order.send(self.lay.lat.swap, part(self.up, self.lay.lat, 1, False))

    def start_near(self, beside=None):
        self.up, self.other = self.order.gate(self.up, self.other)
        own = part(self.up, self.lay.lat, 1, True)
        self.up = pair(self.lay.lat, own, self.other, 1)
        near = self.lay.tensor[0]
        sent = part(self.up, near, 0, False)
        self.beside = beside
        if beside is not None:
            sent = jnp.concatenate([sent.reshape(-1, self.columns), beside], axis=0)
        self.other = self.order.send(near.swap, sent)

    def start_far(self):
        near = self.lay.tensor[0]
        self.up, self.other = self.order.gate(self.up, self.other)
        own = part(self.up, near, 0, True)
        parts = [pair(near, own, self.other.reshape((-1,) + own.shape[1:])[: own.shape[0]], 0)]
        parts.append(self.down)
        if self.beside is not None:
            cut = own.shape[0] * own.shape[1]
            parts.append(pair(near, self.beside, self.other[cut:], 0))
        packed = jnp.concatenate([p.reshape(-1, self.columns) for p in parts], axis=0)
        packed, self.have = join(self.order, packed, self.lay.far[:-1], [])
        self.own = packed
        self.other = self.order.send(self.lay.far[-1].swap, packed)

    def end_far(self):
        place = len(self.have)
        self.own, self.other = self.order.gate(self.own, self.other)
        packed = pair(self.lay.far[-1], self.own, self.other, place)
        self.have = self.have + [self.lay.far[-1]]
        cut = self.rows * self.lay.split
        end = cut + self.down.shape[0]
        up = packed[..., :cut, :]
        self.up = up.reshape((2,) * (len(self.have) + 2) + (self.rows, self.columns))
        self.down = packed[..., cut:end, :]
        if self.beside is not None:
            return packed[..., end:, :].reshape((self.lay.outer, 4) + self.beside.shape)

    def start_plane(self):
        lay = self.lay
        self.up_other = self.order.send(lay.first.swap, self.up)
        self.down_other = self.order.send(lay.second.swap, self.down)

    def gate(self):
        arrays = [self.up, self.up_other, self.down, self.down_other]
        self.up, self.up_other, self.down, self.down_other = self.order.all(arrays)

    def next_plane(self):
        lay = self.lay
        place = len(self.have)
        self.gate()
        self.up = pair(lay.first, self.up, self.up_other, place + 1)
        self.down = pair(lay.second, self.down, self.down_other, place)
        self.up_other = self.order.send(lay.second.swap, self.up)
        self.down_other = self.order.send(lay.first.swap, self.down)

    def end_plane(self):
        lay = self.lay
        place = len(self.have)
        self.gate()
        up = pair(lay.second, self.up, self.up_other, place + 1)
        down = pair(lay.first, self.down, self.down_other, place + 1)
        return up.reshape(-1, self.columns), down.reshape(-1, self.columns)


class FeedGrad:
    def __init__(self, lay, order, up_term, down_term, rows):
        self.lay, self.order, self.rows = lay, order, rows
        self.columns = up_term.shape[1]
        self.up_have = lay.every
        self.up = [up_term.reshape((2,) * len(lay.every) + (rows, self.columns))]
        self.down_have = [bit for bit in lay.every if bit not in lay.tensor]
        self.down = [down_term.reshape((2,) * len(self.down_have) + (-1, self.columns))]

    def plane(self, turn):
        lay = self.lay
        bits = (lay.second, lay.first) if turn == 0 else (lay.first, lay.second)
        self.up, self.up_have = shed(self.order, self.up, bits[0], self.up_have)
        self.down, self.down_have = shed(self.order, self.down, bits[1], self.down_have)

    def settle(self):
        count = len(self.up)
        both = self.order.all(self.up + self.down)
        self.up, self.down = both[:count], both[count:]

    def far(self):
        lay = self.lay
        lead = (2,) * len(lay.far)
        self.settle()
        arrays = [total(self.up), total(self.down)]
        term = jnp.concatenate([a.reshape(lead + (-1, self.columns)) for a in arrays], axis=-2)
        terms, have = [term], list(lay.far)
        for bit in reversed(lay.far):
            terms, have = shed(self.order, terms, bit, have)
        self.terms = terms

    def settle_far(self):
        self.terms = self.order.all(self.terms)

    def take_far(self):
        cut = self.rows * self.lay.split
        packed = total(self.order.all(self.terms))
        self.down = packed[cut:]
        self.up = packed[:cut].astype(BF16).reshape(2, 2, self.rows, self.columns)

    def end(self):
        up = feed_columns(self.lay, self.up.reshape(self.lay.split, self.rows, self.columns), False)
        return up.astype(F32), self.down


def swap_together(lay, order, grads, bit, place):
    sent = jnp.stack([part(grad.up, bit, place, False) for grad in grads])
    return order.send(bit.swap, sent)


def take_together(lay, order, grads, bit, place, others):
    others = order.gate(others)
    for grad, other in zip(grads, others):
        grad.up = pair(bit, part(grad.up, bit, place, True), other, place)


class AttentionGrad:
    def __init__(self, lay, order, left, right):
        self.lay, self.order = lay, order
        self.cut = left.shape[1]
        lead = (lay.outer, 4, 4, 2)
        self.terms = [term.reshape(lead + term.shape[1:]) for term in (left, right)]
        self.tail = None

    def lat(self):
        terms = self.order.all(self.terms)
        lat = self.lay.lat
        sent = jnp.concatenate([part(term, lat, 3, False) for term in terms], axis=-2)
        other = self.order.send(lat.swap, sent)
        own = jnp.concatenate([part(term, lat, 3, True) for term in terms], axis=-2)
        self.terms = [own, other]

    def plane(self, turn, tail=None):
        lay = self.lay
        if turn == 0:
            terms = self.order.all(self.terms)
            width = terms[0].shape[-1]
            cut, rest = self.cut, terms[0].shape[-2] - self.cut
            self.left = [t[..., :cut, :].reshape(-1, 2, 2, cut, width) for t in terms]
            self.right = [t[..., cut:, :].reshape(-1, 2, 2, rest, width) for t in terms]
            places = (1, 2)
        else:
            count = len(self.left)
            terms = self.order.all(self.left + self.right)
            self.left, self.right = terms[:count], terms[count:]
            places = (1, 1)
        bits = (lay.second, lay.first) if turn == 0 else (lay.first, lay.second)
        sent = total([part(term, bits[0], places[0], False) for term in self.left]).astype(BF16)
        own = [part(term, bits[0], places[0], True) for term in self.left]
        if tail is None:
            other = self.order.send(bits[0].swap, sent)
        else:
            tail = tail.astype(BF16)
            rows = sent.size // sent.shape[-1]
            packed = jnp.concatenate([sent.reshape(rows, -1), tail], axis=0)
            packed = self.order.send(bits[0].swap, packed)
            other = packed[:rows].reshape(sent.shape)
            self.tail = [tail, packed[rows:]]
        self.left = own + [other]
        sent = total([part(term, bits[1], places[1], False) for term in self.right]).astype(BF16)
        own = [part(term, bits[1], places[1], True) for term in self.right]
        self.right = own + [self.order.send(bits[1].swap, sent)]

    def join(self):
        count = len(self.left)
        terms = self.order.all(self.left + self.right)
        value = jnp.concatenate([total(terms[:count]), total(terms[count:])], axis=-2)
        return value.reshape((self.lay.outer, 4) + value.shape[-2:])

    def settle(self):
        count = len(self.left)
        terms = self.order.all(self.left + self.right)
        self.left, self.right = terms[:count], terms[count:]

    def column_far(self):
        lay = self.lay
        value = self.join()
        terms, self.have = [value.reshape((2,) * (len(lay.far) + 1) + value.shape[-2:])], lay.far + [lay.tensor[0]]
        for bit in reversed(lay.far):
            terms, self.have = shed(self.order, terms, bit, self.have)
        self.terms = terms

    def column_near(self):
        self.terms, _ = shed(self.order, self.terms, self.lay.tensor[0], self.have)

    def end(self):
        return total(self.order.all(self.terms))

    def column(self):
        value = self.join()
        self.tail = total(self.tail).astype(BF16)
        column = self.lay.column
        me = column.mine()
        self.others = []
        for mask, swap in zip((1, 2, 3), column.swaps):
            sent = pick(value, me ^ mask, 1).astype(BF16)
            sent = jnp.concatenate([sent.reshape(-1, sent.shape[-1]), self.tail], axis=0)
            self.others.append(self.order.send(swap, sent))
        self.own = pick(value, me, 1)

    def finish(self):
        lay = self.lay
        self.own, *others = self.order.all([self.own] + self.others)
        rows = self.own.shape[0] * self.own.shape[1]
        terms = [self.own] + [other[:rows].reshape(self.own.shape) for other in others]
        tails = [self.tail.astype(F32)] + [other[rows:].astype(F32) for other in others]
        tail = (tails[0] + tails[1]) + (tails[2] + tails[3])
        value = total(terms)
        terms = [value.reshape((2,) * len(lay.beyond) + value.shape[1:])]
        have = list(lay.beyond)
        for bit in reversed(lay.beyond):
            terms, have = shed(self.order, terms, bit, have)
        return total(terms), tail


def normalize(rows):
    centered = rows - jnp.mean(rows, axis=-1, keepdims=True)
    rate = lax.rsqrt(jnp.mean(centered * centered, axis=-1, keepdims=True) + 1e-05)
    return centered * rate, rate


def norm_back(grad, rows, gain):
    unit, rate = normalize(rows)
    scaled = grad * gain
    mean = jnp.mean(scaled, axis=-1, keepdims=True)
    along = jnp.mean(scaled * unit, axis=-1, keepdims=True)
    return rate * (scaled - mean - unit * along), jnp.sum(grad * unit, axis=0), jnp.sum(grad, axis=0)


def head_mask(rows, heads, width):
    row = lax.broadcasted_iota(jnp.int32, (heads * rows, width), 0) // rows
    column = lax.broadcasted_iota(jnp.int32, (heads * rows, width), 1) // (width // heads)
    return row == column


def spread_heads(rows, mask, heads):
    return jnp.where(mask, jnp.concatenate([rows] * heads, axis=0), 0)


def merge_heads(array, mask, heads):
    kept = jnp.where(mask, array, 0)
    size = array.shape[0] // heads
    total = kept[:size]
    for head in range(1, heads):
        total = total + kept[head * size : (head + 1) * size]
    return total


def slot_pairs(refs, slot, slots):
    return jnp.concatenate(
        [ref[slot * (ref.shape[0] // slots) : (slot + 1) * (ref.shape[0] // slots)] for ref in refs],
        axis=0,
    )


def soft_scores(query_wide, keys):
    scores = mm_nt(query_wide, keys)
    exponent = jnp.exp(scores - jnp.max(scores, axis=-1, keepdims=True))
    return exponent / jnp.sum(exponent, axis=-1, keepdims=True)


def attend_kernel(slots, heads, spot, refs):
    query, own_m, other_m, own_l, other_l, rows, output_w, norms, mixed, after, normed = refs
    width = query.shape[1]
    count = query.shape[0] // slots
    mask = head_mask(count, heads, width)
    for slot in range(slots):
        pairs = slot_pairs((own_m, other_m, own_l, other_l), slot, slots)
        place = slice(slot * count, (slot + 1) * count)
        wide = spread_heads(query[place] * 0.125, mask, heads)
        probs = soft_scores(wide, pairs[:, :width]).astype(BF16)
        mixed[place] = merge_heads(mm(probs, pairs[:, width:]), mask, heads).astype(BF16)
    total = rows[...] + mm(mixed[...], output_w[...])
    after[...] = total
    unit, _ = normalize(total)
    normed[...] = (unit * norms[spot[0] : spot[0] + 1] + norms[spot[1] : spot[1] + 1]).astype(BF16)


def near_memory(arrays):
    return list(arrays)


def attend(slots, heads, spot, query, own_m, other_m, own_l, other_l, rows, output_w, norms):
    shape = jax.ShapeDtypeStruct
    return pl.pallas_call(
        lambda *refs: attend_kernel(slots, heads, spot, refs),
        out_shape=(
            shape(query.shape, BF16),
            shape(rows.shape, F32),
            shape(rows.shape, BF16),
        ),
        in_specs=[pl.BlockSpec(memory_space=pltpu.VMEM)] * 8,
        out_specs=(pl.BlockSpec(memory_space=pltpu.VMEM),) * 3,
        cost_estimate=LIGHT,
        name="attend",
    )(*near_memory((query, own_m, other_m, own_l, other_l, rows, output_w, norms)))


def attend_back_kernel(slots, heads, spot, refs):
    (
        normed_grad,
        upstream,
        after,
        query,
        own_m,
        other_m,
        own_l,
        other_l,
        mixed,
        output_w,
        norms,
        d_after,
        d_query,
        d_own_m,
        d_other_m,
        d_own_l,
        d_other_l,
        output_grad,
        norm_grad,
    ) = refs
    width = query.shape[1]
    count = query.shape[0] // slots
    mask = head_mask(count, heads, width)
    grad, d_gain, d_shift = norm_back(normed_grad[...], after[...], norms[spot : spot + 1])
    grad = grad + upstream[...]
    d_after[...] = grad
    norm_grad[...] = jnp.zeros_like(norm_grad)
    norm_grad[0:1] = d_gain[None]
    norm_grad[1:2] = d_shift[None]
    low = grad.astype(BF16)
    output_grad[...] = mm_tn(mixed[...], low).astype(BF16)
    mixed_grad = mm_nt(low, output_w[...]).astype(BF16)
    outs = (d_own_m, d_other_m, d_own_l, d_other_l)
    for slot in range(slots):
        pairs = slot_pairs((own_m, other_m, own_l, other_l), slot, slots)
        keys, values = pairs[:, :width], pairs[:, width:]
        place = slice(slot * count, (slot + 1) * count)
        wide = spread_heads(query[place] * 0.125, mask, heads)
        soft = soft_scores(wide, keys)
        wide_grad = spread_heads(mixed_grad[place], mask, heads)
        d_probs = mm_nt(wide_grad, values)
        d_values = mm_tn(soft.astype(BF16), wide_grad).astype(BF16)
        d_scores = soft * (d_probs - jnp.sum(d_probs * soft, axis=-1, keepdims=True))
        d_scores = d_scores.astype(BF16)
        d_keys = mm_tn(d_scores, wide).astype(BF16)
        d_query[place] = (merge_heads(mm(d_scores, keys), mask, heads) * 0.125).astype(BF16)
        start = 0
        for ref in outs:
            size = ref.shape[0] // slots
            ref[slot * size : (slot + 1) * size, :width] = d_keys[start : start + size]
            ref[slot * size : (slot + 1) * size, width:] = d_values[start : start + size]
            start += size


def attend_back(
    slots, heads, spot, normed_grad, upstream, after, query, pairs, mixed, output_w, norms
):
    shape = jax.ShapeDtypeStruct
    own_m, other_m, own_l, other_l = pairs
    return pl.pallas_call(
        lambda *refs: attend_back_kernel(slots, heads, spot, refs),
        out_shape=(
            shape(after.shape, F32),
            shape(query.shape, BF16),
            shape(own_m.shape, BF16),
            shape(other_m.shape, BF16),
            shape(own_l.shape, BF16),
            shape(other_l.shape, BF16),
            shape(output_w.shape, BF16),
            shape((8, after.shape[1]), F32),
        ),
        in_specs=[pl.BlockSpec(memory_space=pltpu.VMEM)] * 11,
        out_specs=(pl.BlockSpec(memory_space=pltpu.VMEM),) * 8,
        cost_estimate=LIGHT,
        name="attend_back",
    )(
        *near_memory(
            (normed_grad, upstream, after, query)
            + (own_m, other_m, own_l, other_l, mixed, output_w, norms)
        )
    )


def media_back_kernel(spot, refs):
    if len(refs) == 7:
        pairs, key_value_w, rows, norms, before, out, norm_grad = refs
    else:
        pairs, key_value_w, rows, norms, out, norm_grad = refs
        before = None

    @pl.when(pl.program_id(0) == 0)
    def _():
        norm_grad[...] = jnp.zeros_like(norm_grad)

    d_norm = mm_nt(pairs[...], key_value_w[...])
    grad, d_gain, d_shift = norm_back(d_norm, rows[...].astype(F32), norms[spot : spot + 1])
    out[...] = grad if before is None else grad + before[...]
    norm_grad[0:1] += d_gain[None]
    norm_grad[1:2] += d_shift[None]


def media_back(slots, spot, pairs, key_value_w, rows, norms, before):
    shape = jax.ShapeDtypeStruct
    block = pl.BlockSpec((rows.shape[0] // slots, rows.shape[1]), lambda i: (i, 0))

    def whole(array):
        return pl.BlockSpec(array.shape, lambda i: (0, 0))

    arrays = [pairs, key_value_w, rows, norms]
    specs = [block, whole(key_value_w), block, whole(norms)]
    if before is not None:
        arrays.append(before)
        specs.append(block)
    return pl.pallas_call(
        lambda *refs: media_back_kernel(spot, refs),
        grid=(slots,),
        out_shape=(shape(rows.shape, F32), shape((8, rows.shape[1]), F32)),
        in_specs=specs,
        out_specs=(block, pl.BlockSpec((8, rows.shape[1]), lambda i: (0, 0))),
        cost_estimate=LIGHT,
        name="media_back",
    )(*arrays)


class Step:
    def __init__(self, lay, order, slots, media_rows, norms, level):
        self.lay, self.order, self.slots = lay, order, slots
        self.media_rows = media_rows
        self.norms = norms
        kinds = 3
        self.gains = [norms[level * kinds + k][None] for k in range(kinds)]
        self.shifts = [norms[(LAYERS + level) * kinds + k][None] for k in range(kinds)]
        self.spot_m = level * kinds
        self.spots = (level * kinds + 2, (LAYERS + level) * kinds + 2)

    def media(self, query_w, key_value_w, output_w):
        self.query_w, self.key_value_w, self.output_w = query_w, key_value_w, output_w
        self.heads = query_w.shape[1] // HEAD
        unit, _ = normalize(self.media_rows.astype(F32))
        self.media_norm = (unit * self.gains[0] + self.shifts[0]).astype(BF16)
        self.own_m = mm(self.media_norm, key_value_w).astype(BF16)
        self.other_m = self.order.send(self.lay.lat.swap, self.own_m)

    def latents(self, rows):
        self.rows = rows
        unit, _ = normalize(rows)
        self.latent_norm = (unit * self.gains[1] + self.shifts[1]).astype(BF16)
        self.own_l = mm(self.latent_norm, self.key_value_w).astype(BF16)
        self.other_l = self.order.send(self.lay.lat.swap, self.own_l)
        self.query = mm(self.latent_norm, self.query_w).astype(BF16)

    def attention(self):
        query, self.other_m, self.other_l = self.order.gate(self.query, self.other_m, self.other_l)
        self.mixed, self.after, self.normed = attend(
            self.slots,
            self.heads,
            self.spots,
            query,
            self.own_m,
            self.other_m,
            self.own_l,
            self.other_l,
            self.rows,
            self.output_w,
            self.norms,
        )

    def feed(self, shared, up_w, down_w):
        self.shared, self.up_w, self.down_w = shared, up_w, down_w
        shared = self.order.gate(shared)
        hidden = mm(shared, up_w)
        big = 0.5 * (1.0 + lax.erf(hidden * (2.0**-0.5)))
        density = jnp.exp(-0.5 * hidden * hidden) * ((2.0 * jnp.pi) ** -0.5)
        self.active = (hidden * big).astype(BF16)
        self.slope = (big + hidden * density).astype(BF16)
        return mm(self.active, down_w).astype(BF16)

    def feed_back(self, branch):
        branch = self.order.gate(branch)
        self.branch = branch
        self.d_hidden = (mm_nt(branch, self.down_w) * self.slope.astype(F32)).astype(BF16)
        return mm_nt(self.d_hidden, self.up_w).astype(BF16)

    def feed_terms(self):
        down = mm_tn(self.active, self.order.gate(self.branch)).astype(BF16)
        up = mm_tn(self.shared, self.d_hidden).astype(BF16)
        rows = up.shape[0] // self.lay.devices
        return FeedGrad(self.lay, self.order, up, down, rows)

    def attention_back(self, normed_grad, upstream):
        normed_grad = self.order.gate(normed_grad)
        (
            self.d_after,
            self.d_query,
            self.d_own_m,
            d_other_m,
            self.d_own_l,
            d_other_l,
            self.output_term,
            self.feed_norm,
        ) = attend_back(
            self.slots,
            self.heads,
            self.spots[0],
            normed_grad,
            upstream,
            self.after,
            self.query,
            (self.own_m, self.other_m, self.own_l, self.other_l),
            self.mixed,
            self.output_w,
            self.norms,
        )
        self.back_l = self.order.send(self.lay.lat.swap, d_other_l)
        self.back_m = self.order.send(self.lay.lat.swap, d_other_m)

    def latents_back(self):
        pairs_l = total(self.order.gate(self.d_own_l, self.back_l)).astype(BF16)
        self.pairs_l = pairs_l
        d_norm = mm_nt(pairs_l, self.key_value_w) + mm_nt(self.d_query, self.query_w)
        d_rows, self.gain_l, self.shift_l = norm_back(d_norm, self.rows, self.gains[1])
        return d_rows + self.d_after

    def attention_terms(self):
        lay = self.lay
        latent_norm = self.order.gate(self.latent_norm)
        width = self.output_w.shape[1]
        half = width // 2
        query = mm_tn(latent_norm, self.d_query).astype(BF16)
        query = query.reshape(lay.devices, -1, half)
        output = self.output_term.reshape(lay.devices, -1, width)
        output = jnp.concatenate([output[..., :half], output[..., half:]], axis=1)
        right = jnp.concatenate([query, output], axis=-1)
        self.pairs_m = total(self.order.gate(self.d_own_m, self.back_m)).astype(BF16)
        pairs_m = self.pairs_m
        left = (mm_tn(self.media_norm, pairs_m) + mm_tn(self.latent_norm, self.pairs_l)).astype(BF16)
        left = left.reshape(lay.devices, -1, width)
        return AttentionGrad(lay, self.order, left, right)

    def media_back(self, before):
        pairs_m = self.order.gate(self.pairs_m)
        d_media, grads = media_back(
            self.slots, self.spot_m, pairs_m, self.key_value_w, self.media_rows, self.norms, before
        )
        self.norm_m = grads
        return self.order.gate(d_media)

    def norm_terms(self):
        norm_m = self.order.gate(self.norm_m)
        self.gain_m, self.shift_m = norm_m[0], norm_m[1]
        gains = [self.gain_m, self.gain_l, self.feed_norm[0]]
        shifts = [self.shift_m, self.shift_l, self.feed_norm[1]]
        return gains, shifts


def gather_near(lay, order, rows):
    return rows, order.send(lay.tensor[0].swap, rows)


def gather_lat(lay, order, pieces):
    rows = jnp.concatenate(order.all(pieces), axis=0)
    return rows, order.send(lay.lat.swap, rows)


def return_lat(lay, order, rows):
    half = rows.shape[0] // 2
    return rows[:half], order.send(lay.lat.swap, rows[half:])


def return_near(lay, order, terms):
    half = terms[0].shape[0] // 2
    terms = order.all(terms)
    sent = total([term[half:] for term in terms]).astype(BF16)
    return [term[:half] for term in terms] + [order.send(lay.tensor[0].swap, sent)]


def make_device(lay):
    def per_device(
        media_tokens,
        image_counts,
        latent_init,
        cotangent,
        query_weight,
        key_value_weight,
        output_weight,
        up_weight,
        down_weight,
        norm_gain,
        norm_shift,
    ):
        first = norm_gain[0, :1].astype(F32)
        order = Order(first)
        slots = media_tokens.shape[0]
        model = media_tokens.shape[2]
        count = latent_init.shape[0]
        position = jnp.arange(slots) % MEDIA
        per_slot = jnp.repeat(image_counts, MEDIA)
        valid = (position < per_slot).astype(F32)[:, None, None]
        row_mask = jnp.broadcast_to(valid, (slots, count, 1)).reshape(-1, 1)
        media_rows = media_tokens.reshape(-1, model)
        device = lax.axis_index("img") * lax.axis_size("lat") + lax.axis_index("lat")
        lanes = norm_gain.shape[-1]
        kinds = norm_gain.shape[1]
        norms = jnp.concatenate(
            [norm_gain.reshape(-1, lanes), norm_shift.reshape(-1, lanes)], axis=0
        )
        spread = jnp.zeros((NORM_ROWS, model), BF16)
        spread = lax.dynamic_update_slice(spread, norms, (0, device * lanes))
        attn = [
            Attention(
                lay,
                order,
                key_value_weight[level],
                output_weight[level],
                query_weight[level],
                spread if level == 0 else None,
            )
            for level in range(LAYERS)
        ]
        feed = [Feed(lay, order, up_weight[level], down_weight[level]) for level in range(LAYERS)]
        upstream = cotangent.astype(F32).reshape(-1, model) * row_mask

        attn[0].start_column()
        feed[0].start_lat()
        feed[0].start_near()
        attn[0].end_column()
        attn[0].start_plane()
        feed[0].start_far()
        feed[1].start_lat()
        feed[1].start_near(attn[1].own)
        feed[0].end_far()
        attn[0].end_plane()
        attn[0].start_lat()
        feed[0].start_plane()
        feed[1].start_far()
        weights = attn[0].end_lat()
        step0 = Step(lay, order, slots, media_rows, attn[0].norms, 0)
        step0.media(*weights)
        rows0 = jnp.broadcast_to(latent_init.astype(F32), (slots, count, model)).reshape(-1, model)
        feed[0].next_plane()
        step0.latents(rows0)
        step0.attention()
        pieces = gather_near(lay, order, step0.normed)
        pieces = gather_lat(lay, order, pieces)
        feed_w = feed[0].end_plane()
        attn[1].own = feed[1].end_far()
        attn[1].start_plane()
        out = step0.feed(jnp.concatenate(order.all(pieces), axis=0), *feed_w)
        terms = return_lat(lay, order, out)
        attn[1].end_plane()
        attn[1].start_lat()
        feed[1].start_plane()
        weights = attn[1].end_lat()
        terms = return_near(lay, order, terms)
        step1 = Step(lay, order, slots, media_rows, attn[0].norms, 1)
        step1.media(*weights)
        feed[1].next_plane()
        rows1 = step0.after + total(order.all(terms))
        step1.latents(rows1)
        branch = gather_near(lay, order, upstream.astype(BF16))
        step1.attention()
        pieces = gather_near(lay, order, step1.normed)
        branch = gather_lat(lay, order, branch)
        pieces = gather_lat(lay, order, pieces)
        feed_w = feed[1].end_plane()
        out = step1.feed(jnp.concatenate(order.all(pieces), axis=0), *feed_w)
        terms_out = return_lat(lay, order, out)
        out = step1.feed_back(jnp.concatenate(order.all(branch), axis=0))
        terms = return_lat(lay, order, out)
        feed_grad1 = step1.feed_terms()
        terms = return_near(lay, order, terms)
        feed_grad1.plane(0)
        step1.attention_back(total(order.all(terms)), upstream)
        terms_out = return_near(lay, order, terms_out)
        upstream0 = step1.latents_back()
        branch = gather_near(lay, order, upstream0.astype(BF16))
        feed_grad1.plane(1)
        branch = gather_lat(lay, order, branch)
        attn_grad1 = step1.attention_terms()
        out = step0.feed_back(jnp.concatenate(order.all(branch), axis=0))
        terms = return_lat(lay, order, out)
        attn_grad1.lat()
        terms = return_near(lay, order, terms)
        feed_grad0 = step0.feed_terms()
        feed_grad1.settle()
        attn_grad1.plane(0)
        feed_grad0.plane(0)
        normed_grad = total(order.all(terms))
        feed_grad1.far()
        attn_grad1.settle()
        step0.attention_back(normed_grad, upstream0)
        last = step0.latents_back()
        feed_grad0.plane(1)
        feed_grad1.settle_far()
        attn_grad0 = step0.attention_terms()
        attn_grad0.lat()
        attn_grad1.plane(1)
        feed_grad0.far()
        attn_grad0.plane(0)
        media1 = step1.media_back(None)
        media_grad = step0.media_back(media1)
        attn_grad1.settle()
        attn_grad0.settle()
        feed_grad0.settle_far()
        gains0, shifts0 = step0.norm_terms()
        gains1, shifts1 = step1.norm_terms()
        small = jnp.stack(gains0 + gains1 + shifts0 + shifts1)
        small = jnp.pad(small, ((0, NORM_ROWS - small.shape[0]), (0, 0)))
        latent = jnp.sum(last.reshape(slots, count, model), axis=0)
        tail = jnp.concatenate([latent, small], axis=0)
        tail = order.gate(tail).astype(BF16)
        tail = [tail, order.send(lay.second.swap, tail)]
        attn_grad1.column_far()
        grads = [feed_grad0, feed_grad1]
        for grad in grads:
            grad.take_far()
        near, lat = lay.tensor
        others = swap_together(lay, order, grads, near, 0)
        attn_grad0.plane(1, total(order.all(tail)))
        take_together(lay, order, grads, near, 0, others)
        others = swap_together(lay, order, grads, lat, 1)
        attn_grad1.column_near()
        attn_grad0.column()
        take_together(lay, order, grads, lat, 1, others)
        end0, tail = attn_grad0.finish()
        for bit in lay.img[4:]:
            tail = tail + order.send(bit.swap, tail)
        small = tail[count:]
        small = small + order.send(lay.lat.swap, small)
        small = lax.dynamic_slice(small, (0, device * lanes), (2 * LAYERS * kinds, lanes))
        ends = [end0, attn_grad1.end()]
        small = small + (order.token - first)
        small = small.reshape(2, LAYERS, kinds, lanes)
        cut = key_value_weight.shape[1]
        lefts = [entry[:cut] for entry in ends]
        rights = [entry[cut:] for entry in ends]
        feeds = [feed_grad0.end(), feed_grad1.end()]
        half = model // 2
        outs = []
        for right in rights:
            cut = right.shape[0] // 2
            outs.append(jnp.concatenate([right[:cut, half:], right[cut:, half:]], axis=1))
        resampled = ((step1.after + total(terms_out)) * row_mask).reshape(cotangent.shape)
        return (
            resampled,
            media_grad.reshape(media_tokens.shape),
            tail[:count],
            jnp.stack([right[:, :half] for right in rights]),
            jnp.stack(lefts),
            jnp.stack(outs),
            jnp.stack([entry[0] for entry in feeds]),
            jnp.stack([entry[1] for entry in feeds]),
            small[0],
            small[1],
        )

    return per_device


def solution(mesh):
    lay = Layout(mesh.shape["img"], mesh.shape["lat"])
    in_specs = (
        P("img", "lat", None),
        P("img"),
        P("lat", None),
        P("img", "lat", None),
        P(None, ("img", "lat"), None),
        P(None, ("img", "lat"), None),
        P(None, ("img", "lat"), None),
        P(None, ("img", "lat"), None),
        P(None, ("img", "lat"), None),
        P(None, None, ("img", "lat")),
        P(None, None, ("img", "lat")),
    )
    out_specs = (
        P("img", "lat", None),
        P("img", "lat", None),
        P("lat", None),
        P(None, ("img", "lat"), None),
        P(None, ("img", "lat"), None),
        P(None, ("img", "lat"), None),
        P(None, ("img", "lat"), None),
        P(None, ("img", "lat"), None),
        P(None, None, ("img", "lat")),
        P(None, None, ("img", "lat")),
    )
    return jax.shard_map(
        make_device(lay), mesh=mesh, in_specs=in_specs, out_specs=out_specs, check_vma=False
    )
```

```python
import jax
import jax.numpy as jnp
from jax import lax
from jax.experimental import pallas as pl
from jax.experimental.pallas import tpu as pltpu
from jax.sharding import PartitionSpec as P

HEAD = 64
MEDIA = 5
LAYERS = 2
F32 = jnp.float32
BF16 = jnp.bfloat16
NORM_ROWS = 16
LIGHT = pl.CostEstimate(flops=1, bytes_accessed=1, transcendentals=0)


class Order:
    def __init__(self, token):
        self.token = token

    def gate(self, *arrays):
        arrays = lax.optimization_barrier(arrays + (self.token,))
        self.token = arrays[-1]
        return arrays[:-1] if len(arrays) > 2 else arrays[0]

    def all(self, arrays):
        arrays = lax.optimization_barrier(tuple(arrays) + (self.token,))
        self.token = arrays[-1]
        return list(arrays[:-1])

    def send(self, swap, array):
        return swap(self.gate(array))


class Bit:
    def __init__(self, axis, size, place, rank):
        self.rank = rank
        self.axis = axis
        self.mask = 1 << place
        self.pairs = [(source, source ^ self.mask) for source in range(size)]

    def mine(self):
        return (lax.axis_index(self.axis) // self.mask) % 2

    def swap(self, array):
        return lax.ppermute(array, self.axis, self.pairs)


class Four:
    def __init__(self, size, place):
        self.shift = 1 << place
        self.swaps = [self._swap(size, mask) for mask in (1, 2, 3)]

    def _swap(self, size, mask):
        pairs = [(source, source ^ (mask * self.shift)) for source in range(size)]
        return lambda array: lax.ppermute(array, "img", pairs)

    def mine(self):
        return (lax.axis_index("img") // self.shift) % 4

    def spread(self, order, array):
        return [order.send(swap, array) for swap in self.swaps]

    def merge(self, own, others, axis):
        pieces = [own] + others
        low = self.mine() % 2 == 0
        high = self.mine() // 2 == 0
        mixed = [
            [jnp.where(low, pieces[2 * a + b], pieces[2 * a + 1 - b]) for b in range(2)]
            for a in range(2)
        ]
        return jnp.stack(
            [jnp.where(high, mixed[c][b], mixed[1 - c][b]) for c in range(2) for b in range(2)],
            axis=axis,
        )

    def add(self, order, array, others):
        array, *others = order.all([array] + others)
        return (array + others[0]) + (others[1] + others[2])

    def shed(self, order, terms, axis):
        me = self.mine()
        terms = list(order.all(terms))
        others = []
        for mask, swap in zip((1, 2, 3), self.swaps):
            sent = total([pick(term, me ^ mask, axis) for term in terms]).astype(BF16)
            others.append(order.send(swap, sent))
        return [pick(term, me, axis) for term in terms] + others


class Layout:
    def __init__(self, img, lat):
        lat_bits = [Bit("lat", lat, k, k) for k in range(lat.bit_length() - 1)]
        img_bits = [Bit("img", img, k, k + len(lat_bits)) for k in range(img.bit_length() - 1)]
        self.devices = img * lat
        self.lat = lat_bits[0]
        self.img = img_bits
        self.every = list(reversed(lat_bits + img_bits))
        self.first, self.second = img_bits[0], img_bits[1]
        self.far = list(reversed(img_bits[3:]))
        self.beyond = list(reversed(img_bits[4:]))
        self.plane = Four(img, 0)
        self.column = Four(img, 2)
        self.tensor = [img_bits[2], lat_bits[0]]
        self.split = 4
        self.outer = img // 16


def pick(array, index, axis):
    return lax.dynamic_index_in_dim(array, index, axis, keepdims=False)


def part(array, bit, place, own):
    return pick(array, bit.mine() if own else 1 - bit.mine(), place)


def pair(bit, own, other, axis):
    low = bit.mine() == 0
    return jnp.stack([jnp.where(low, own, other), jnp.where(low, other, own)], axis=axis)


def join(order, array, bits, have):
    have = list(have)
    for bit in bits:
        other = order.send(bit.swap, array)
        place = sum(1 for held in have if held.rank > bit.rank)
        array = pair(bit, array, other, place)
        have.insert(place, bit)
    return array, have


def total(terms):
    value = terms[0].astype(F32)
    for term in terms[1:]:
        value = value + term.astype(F32)
    return value


def shed(order, terms, bit, have):
    place = have.index(bit)
    terms = order.all(terms)
    sent = total([part(term, bit, place, False) for term in terms]).astype(BF16)
    other = order.send(bit.swap, sent)
    terms = [part(term, bit, place, True) for term in terms] + [other]
    return terms, [held for held in have if held is not bit]


def exchange(order, array, bit, place):
    other = order.send(bit.swap, part(array, bit, place, False))
    return pair(bit, part(array, bit, place, True), other, place)


def mm(a, b):
    return lax.dot_general(a, b, (((1,), (0,)), ((), ())), preferred_element_type=F32)


def mm_nt(a, b):
    return lax.dot_general(a, b, (((1,), (1,)), ((), ())), preferred_element_type=F32)


def mm_tn(a, b):
    return lax.dot_general(a, b, (((0,), (0,)), ((), ())), preferred_element_type=F32)


class Attention:
    def __init__(self, lay, order, kv_shard, out_shard, query_shard, extra):
        self.lay, self.order = lay, order
        self.rows, self.width = kv_shard.shape
        self.out_rows = out_shard.shape[0]
        half = self.width // 2
        outs = jnp.concatenate([out_shard[:, :half], out_shard[:, half:]], axis=0)
        parts = [kv_shard, jnp.concatenate([query_shard, outs], axis=1)]
        if extra is not None:
            parts.append(extra)
        self.extra = extra is not None
        self.own = jnp.concatenate(parts, axis=0)

    def start_column(self):
        lay = self.lay
        self.own, _ = join(self.order, self.own, lay.beyond, [])
        self.own = self.own.reshape((lay.outer,) + self.own.shape[-2:])
        self.others = lay.column.spread(self.order, self.own)

    def end_column(self):
        own, *others = self.order.all([self.own] + self.others)
        self.own = self.lay.column.merge(own, others, 1)

    def start_plane(self):
        self.others = self.lay.plane.spread(self.order, self.own)

    def end_plane(self):
        own, *others = self.order.all([self.own] + self.others)
        self.own = self.lay.plane.merge(own, others, 2)

    def start_lat(self):
        self.others = self.order.send(self.lay.lat.swap, self.own)

    def end_lat(self):
        lay, rows, width = self.lay, self.rows, self.width
        half = width // 2
        self.own, self.others = self.order.gate(self.own, self.others)

        def both(select):
            return pair(lay.lat, select(self.own), select(self.others), 3)

        key_value = both(lambda a: a[..., :rows, :]).reshape(-1, width)
        query = both(lambda a: a[..., rows : 2 * rows, :half]).reshape(-1, half)
        middle = rows + self.out_rows
        output = both(
            lambda a: jnp.concatenate(
                [a[..., rows:middle, half:], a[..., middle : 2 * rows, half:]], axis=-1
            )
        ).reshape(-1, width)
        if self.extra:
            own = self.own[..., 2 * rows :, :].astype(F32)
            other = self.others[..., 2 * rows :, :].astype(F32)
            self.norms = jnp.sum(own, axis=(0, 1, 2)) + jnp.sum(other, axis=(0, 1, 2))
        return query, key_value, output


def feed_columns(lay, array, forward):
    width = array.shape[-1] // lay.devices if forward else None
    ranks = [bit.rank for bit in lay.tensor]
    owner = []
    for device in range(lay.devices):
        value = 0
        for rank in ranks:
            value = value * 2 + (device >> rank) % 2
        owner.append(value)
    if forward:
        blocks = [array[..., d * width : (d + 1) * width] for d in range(lay.devices)]
        sets = [
            jnp.concatenate([blocks[d] for d in range(lay.devices) if owner[d] == s], axis=-1)
            for s in range(lay.split)
        ]
        return jnp.stack(sets)
    width = array.shape[-1] * lay.split // lay.devices
    seen = [0] * lay.split
    blocks = []
    for device in range(lay.devices):
        s = owner[device]
        blocks.append(array[s, :, seen[s] * width : (seen[s] + 1) * width])
        seen[s] += 1
    return jnp.concatenate(blocks, axis=-1)


class Feed:
    def __init__(self, lay, order, up_shard, down_shard):
        self.lay, self.order = lay, order
        self.rows = up_shard.shape[0]
        self.columns = up_shard.shape[1] // lay.split
        up = feed_columns(lay, up_shard, True)
        self.up = up.reshape((2, 2, self.rows, self.columns))
        self.down = down_shard

    def start_lat(self):
        self.other = self.order.send(self.lay.lat.swap, part(self.up, self.lay.lat, 1, False))

    def start_near(self, beside=None):
        self.up, self.other = self.order.gate(self.up, self.other)
        own = part(self.up, self.lay.lat, 1, True)
        self.up = pair(self.lay.lat, own, self.other, 1)
        near = self.lay.tensor[0]
        sent = part(self.up, near, 0, False)
        self.beside = beside
        if beside is not None:
            sent = jnp.concatenate([sent.reshape(-1, self.columns), beside], axis=0)
        self.other = self.order.send(near.swap, sent)

    def end_near(self):
        near = self.lay.tensor[0]
        self.up, self.other = self.order.gate(self.up, self.other)
        own = part(self.up, near, 0, True)
        parts = [pair(near, own, self.other.reshape((-1,) + own.shape[1:])[: own.shape[0]], 0)]
        parts.append(self.down)
        if self.beside is not None:
            cut = own.shape[0] * own.shape[1]
            parts.append(pair(near, self.beside, self.other[cut:], 0))
        self.own = jnp.concatenate([p.reshape(-1, self.columns) for p in parts], axis=0)

    def start_far(self):
        packed, self.have = join(self.order, self.own, self.lay.far[:-1], [])
        self.own = packed
        self.other = self.order.send(self.lay.far[-1].swap, packed)

    def end_far(self):
        place = len(self.have)
        self.own, self.other = self.order.gate(self.own, self.other)
        packed = pair(self.lay.far[-1], self.own, self.other, place)
        self.have = self.have + [self.lay.far[-1]]
        cut = self.rows * self.lay.split
        end = cut + self.down.shape[0]
        up = packed[..., :cut, :]
        self.up = up.reshape((2,) * (len(self.have) + 2) + (self.rows, self.columns))
        self.down = packed[..., cut:end, :]
        if self.beside is not None:
            return packed[..., end:, :].reshape((self.lay.outer, 4) + self.beside.shape)

    def start_plane(self):
        lay = self.lay
        self.up_other = self.order.send(lay.first.swap, self.up)
        self.down_other = self.order.send(lay.second.swap, self.down)

    def gate(self):
        arrays = [self.up, self.up_other, self.down, self.down_other]
        self.up, self.up_other, self.down, self.down_other = self.order.all(arrays)

    def next_plane(self):
        lay = self.lay
        place = len(self.have)
        self.gate()
        self.up = pair(lay.first, self.up, self.up_other, place + 1)
        self.down = pair(lay.second, self.down, self.down_other, place)
        self.up_other = self.order.send(lay.second.swap, self.up)
        self.down_other = self.order.send(lay.first.swap, self.down)

    def end_plane(self):
        lay = self.lay
        place = len(self.have)
        self.gate()
        up = pair(lay.second, self.up, self.up_other, place + 1)
        down = pair(lay.first, self.down, self.down_other, place + 1)
        return up.reshape(-1, self.columns), down.reshape(-1, self.columns)


class FeedGrad:
    def __init__(self, lay, order, up_term, down_term, rows):
        self.lay, self.order, self.rows = lay, order, rows
        self.columns = up_term.shape[1]
        self.up_have = lay.every
        self.up = [up_term.reshape((2,) * len(lay.every) + (rows, self.columns))]
        self.down_have = [bit for bit in lay.every if bit not in lay.tensor]
        self.down = [down_term.reshape((2,) * len(self.down_have) + (-1, self.columns))]

    def plane(self, turn):
        lay = self.lay
        bits = (lay.second, lay.first) if turn == 0 else (lay.first, lay.second)
        self.up, self.up_have = shed(self.order, self.up, bits[0], self.up_have)
        self.down, self.down_have = shed(self.order, self.down, bits[1], self.down_have)

    def settle(self):
        count = len(self.up)
        both = self.order.all(self.up + self.down)
        self.up, self.down = both[:count], both[count:]

    def far(self):
        lay = self.lay
        lead = (2,) * len(lay.far)
        self.settle()
        arrays = [total(self.up), total(self.down)]
        term = jnp.concatenate([a.reshape(lead + (-1, self.columns)) for a in arrays], axis=-2)
        terms, have = [term], list(lay.far)
        for bit in reversed(lay.far):
            terms, have = shed(self.order, terms, bit, have)
        self.terms = terms

    def settle_far(self):
        self.terms = self.order.all(self.terms)

    def take_far(self):
        cut = self.rows * self.lay.split
        packed = total(self.order.all(self.terms))
        self.down = packed[cut:]
        self.up = packed[:cut].astype(BF16).reshape(2, 2, self.rows, self.columns)

    def end(self):
        up = feed_columns(self.lay, self.up.reshape(self.lay.split, self.rows, self.columns), False)
        return up.astype(F32), self.down


def swap_together(lay, order, grads, bit, place):
    sent = jnp.stack([part(grad.up, bit, place, False) for grad in grads])
    return order.send(bit.swap, sent)


def take_together(lay, order, grads, bit, place, others):
    others = order.gate(others)
    for grad, other in zip(grads, others):
        grad.up = pair(bit, part(grad.up, bit, place, True), other, place)


class AttentionGrad:
    def __init__(self, lay, order, left, right):
        self.lay, self.order = lay, order
        self.cut = left.shape[1]
        lead = (lay.outer, 4, 4, 2)
        self.terms = [term.reshape(lead + term.shape[1:]) for term in (left, right)]
        self.tail = None

    def lat(self):
        terms = self.order.all(self.terms)
        lat = self.lay.lat
        sent = jnp.concatenate([part(term, lat, 3, False) for term in terms], axis=-2)
        other = self.order.send(lat.swap, sent)
        own = jnp.concatenate([part(term, lat, 3, True) for term in terms], axis=-2)
        self.terms = [own, other]

    def plane(self, turn, tail=None):
        lay = self.lay
        if turn == 0:
            terms = self.order.all(self.terms)
            width = terms[0].shape[-1]
            cut, rest = self.cut, terms[0].shape[-2] - self.cut
            self.left = [t[..., :cut, :].reshape(-1, 2, 2, cut, width) for t in terms]
            self.right = [t[..., cut:, :].reshape(-1, 2, 2, rest, width) for t in terms]
            places = (1, 2)
        else:
            count = len(self.left)
            terms = self.order.all(self.left + self.right)
            self.left, self.right = terms[:count], terms[count:]
            places = (1, 1)
        bits = (lay.second, lay.first) if turn == 0 else (lay.first, lay.second)
        sent = total([part(term, bits[0], places[0], False) for term in self.left]).astype(BF16)
        own = [part(term, bits[0], places[0], True) for term in self.left]
        if tail is None:
            other = self.order.send(bits[0].swap, sent)
        else:
            tail = tail.astype(BF16)
            rows = sent.size // sent.shape[-1]
            packed = jnp.concatenate([sent.reshape(rows, -1), tail], axis=0)
            packed = self.order.send(bits[0].swap, packed)
            other = packed[:rows].reshape(sent.shape)
            self.tail = [tail, packed[rows:]]
        self.left = own + [other]
        sent = total([part(term, bits[1], places[1], False) for term in self.right]).astype(BF16)
        own = [part(term, bits[1], places[1], True) for term in self.right]
        self.right = own + [self.order.send(bits[1].swap, sent)]

    def join(self):
        count = len(self.left)
        terms = self.order.all(self.left + self.right)
        value = jnp.concatenate([total(terms[:count]), total(terms[count:])], axis=-2)
        return value.reshape((self.lay.outer, 4) + value.shape[-2:])

    def settle(self):
        count = len(self.left)
        terms = self.order.all(self.left + self.right)
        self.left, self.right = terms[:count], terms[count:]

    def column_far(self):
        lay = self.lay
        value = self.join()
        terms, self.have = [value.reshape((2,) * (len(lay.far) + 1) + value.shape[-2:])], lay.far + [lay.tensor[0]]
        for bit in reversed(lay.far):
            terms, self.have = shed(self.order, terms, bit, self.have)
        self.terms = terms

    def column_near(self):
        self.terms, _ = shed(self.order, self.terms, self.lay.tensor[0], self.have)

    def end(self):
        return total(self.order.all(self.terms))

    def column(self):
        value = self.join()
        self.tail = total(self.tail).astype(BF16)
        column = self.lay.column
        me = column.mine()
        self.others = []
        for mask, swap in zip((1, 2, 3), column.swaps):
            sent = pick(value, me ^ mask, 1).astype(BF16)
            sent = jnp.concatenate([sent.reshape(-1, sent.shape[-1]), self.tail], axis=0)
            self.others.append(self.order.send(swap, sent))
        self.own = pick(value, me, 1)

    def finish(self):
        lay = self.lay
        self.own, *others = self.order.all([self.own] + self.others)
        rows = self.own.shape[0] * self.own.shape[1]
        terms = [self.own] + [other[:rows].reshape(self.own.shape) for other in others]
        tails = [self.tail.astype(F32)] + [other[rows:].astype(F32) for other in others]
        tail = (tails[0] + tails[1]) + (tails[2] + tails[3])
        value = total(terms)
        terms = [value.reshape((2,) * len(lay.beyond) + value.shape[1:])]
        have = list(lay.beyond)
        for bit in reversed(lay.beyond):
            terms, have = shed(self.order, terms, bit, have)
        return total(terms), tail


def normalize(rows):
    centered = rows - jnp.mean(rows, axis=-1, keepdims=True)
    rate = lax.rsqrt(jnp.mean(centered * centered, axis=-1, keepdims=True) + 1e-05)
    return centered * rate, rate


def norm_back(grad, rows, gain):
    unit, rate = normalize(rows)
    scaled = grad * gain
    mean = jnp.mean(scaled, axis=-1, keepdims=True)
    along = jnp.mean(scaled * unit, axis=-1, keepdims=True)
    return rate * (scaled - mean - unit * along), jnp.sum(grad * unit, axis=0), jnp.sum(grad, axis=0)


def head_mask(rows, heads, width):
    row = lax.broadcasted_iota(jnp.int32, (heads * rows, width), 0) // rows
    column = lax.broadcasted_iota(jnp.int32, (heads * rows, width), 1) // (width // heads)
    return row == column


def spread_heads(rows, mask, heads):
    return jnp.where(mask, jnp.concatenate([rows] * heads, axis=0), 0)


def merge_heads(array, mask, heads):
    kept = jnp.where(mask, array, 0)
    size = array.shape[0] // heads
    total = kept[:size]
    for head in range(1, heads):
        total = total + kept[head * size : (head + 1) * size]
    return total


def slot_pairs(refs, slot, slots):
    return jnp.concatenate(
        [ref[slot * (ref.shape[0] // slots) : (slot + 1) * (ref.shape[0] // slots)] for ref in refs],
        axis=0,
    )


def soft_scores(query_wide, keys):
    scores = mm_nt(query_wide, keys)
    exponent = jnp.exp(scores - jnp.max(scores, axis=-1, keepdims=True))
    return exponent / jnp.sum(exponent, axis=-1, keepdims=True)


def attend_kernel(slots, heads, spot, refs):
    query, own_m, other_m, own_l, other_l, rows, output_w, norms, mixed, after, normed = refs
    width = query.shape[1]
    count = query.shape[0] // slots
    mask = head_mask(count, heads, width)
    for slot in range(slots):
        pairs = slot_pairs((own_m, other_m, own_l, other_l), slot, slots)
        place = slice(slot * count, (slot + 1) * count)
        wide = spread_heads(query[place] * 0.125, mask, heads)
        probs = soft_scores(wide, pairs[:, :width]).astype(BF16)
        mixed[place] = merge_heads(mm(probs, pairs[:, width:]), mask, heads).astype(BF16)
    total = rows[...] + mm(mixed[...], output_w[...])
    after[...] = total
    unit, _ = normalize(total)
    normed[...] = (unit * norms[spot[0] : spot[0] + 1] + norms[spot[1] : spot[1] + 1]).astype(BF16)


def near_memory(arrays):
    return list(arrays)


def attend(slots, heads, spot, query, own_m, other_m, own_l, other_l, rows, output_w, norms):
    shape = jax.ShapeDtypeStruct
    return pl.pallas_call(
        lambda *refs: attend_kernel(slots, heads, spot, refs),
        out_shape=(
            shape(query.shape, BF16),
            shape(rows.shape, F32),
            shape(rows.shape, BF16),
        ),
        in_specs=[pl.BlockSpec(memory_space=pltpu.VMEM)] * 8,
        out_specs=(pl.BlockSpec(memory_space=pltpu.VMEM),) * 3,
        cost_estimate=LIGHT,
        name="attend",
    )(*near_memory((query, own_m, other_m, own_l, other_l, rows, output_w, norms)))


def attend_back_kernel(slots, heads, spot, refs):
    (
        normed_grad,
        upstream,
        after,
        query,
        own_m,
        other_m,
        own_l,
        other_l,
        mixed,
        output_w,
        norms,
        d_after,
        d_query,
        d_own_m,
        d_other_m,
        d_own_l,
        d_other_l,
        output_grad,
        norm_grad,
    ) = refs
    width = query.shape[1]
    count = query.shape[0] // slots
    mask = head_mask(count, heads, width)
    grad, d_gain, d_shift = norm_back(normed_grad[...], after[...], norms[spot : spot + 1])
    grad = grad + upstream[...]
    d_after[...] = grad
    norm_grad[...] = jnp.zeros_like(norm_grad)
    norm_grad[0:1] = d_gain[None]
    norm_grad[1:2] = d_shift[None]
    low = grad.astype(BF16)
    output_grad[...] = mm_tn(mixed[...], low).astype(BF16)
    mixed_grad = mm_nt(low, output_w[...]).astype(BF16)
    outs = (d_own_m, d_other_m, d_own_l, d_other_l)
    for slot in range(slots):
        pairs = slot_pairs((own_m, other_m, own_l, other_l), slot, slots)
        keys, values = pairs[:, :width], pairs[:, width:]
        place = slice(slot * count, (slot + 1) * count)
        wide = spread_heads(query[place] * 0.125, mask, heads)
        soft = soft_scores(wide, keys)
        wide_grad = spread_heads(mixed_grad[place], mask, heads)
        d_probs = mm_nt(wide_grad, values)
        d_values = mm_tn(soft.astype(BF16), wide_grad).astype(BF16)
        d_scores = soft * (d_probs - jnp.sum(d_probs * soft, axis=-1, keepdims=True))
        d_scores = d_scores.astype(BF16)
        d_keys = mm_tn(d_scores, wide).astype(BF16)
        d_query[place] = (merge_heads(mm(d_scores, keys), mask, heads) * 0.125).astype(BF16)
        start = 0
        for ref in outs:
            size = ref.shape[0] // slots
            ref[slot * size : (slot + 1) * size, :width] = d_keys[start : start + size]
            ref[slot * size : (slot + 1) * size, width:] = d_values[start : start + size]
            start += size


def attend_back(
    slots, heads, spot, normed_grad, upstream, after, query, pairs, mixed, output_w, norms
):
    shape = jax.ShapeDtypeStruct
    own_m, other_m, own_l, other_l = pairs
    return pl.pallas_call(
        lambda *refs: attend_back_kernel(slots, heads, spot, refs),
        out_shape=(
            shape(after.shape, F32),
            shape(query.shape, BF16),
            shape(own_m.shape, BF16),
            shape(other_m.shape, BF16),
            shape(own_l.shape, BF16),
            shape(other_l.shape, BF16),
            shape(output_w.shape, BF16),
            shape((8, after.shape[1]), F32),
        ),
        in_specs=[pl.BlockSpec(memory_space=pltpu.VMEM)] * 11,
        out_specs=(pl.BlockSpec(memory_space=pltpu.VMEM),) * 8,
        cost_estimate=LIGHT,
        name="attend_back",
    )(
        *near_memory(
            (normed_grad, upstream, after, query)
            + (own_m, other_m, own_l, other_l, mixed, output_w, norms)
        )
    )


def media_back_kernel(spots, refs):
    layers = len(spots)
    pairs, weights = refs[:layers], refs[layers : 2 * layers]
    rows, norms, out, norm_grad = refs[2 * layers :]

    @pl.when(pl.program_id(0) == 0)
    def _():
        norm_grad[...] = jnp.zeros_like(norm_grad)

    unit, rate = normalize(rows[...].astype(F32))
    scaled = None
    for level in range(layers):
        grad = mm_nt(pairs[level][...], weights[level][...])
        norm_grad[level : level + 1] += jnp.sum(grad * unit, axis=0)[None]
        norm_grad[layers + level : layers + level + 1] += jnp.sum(grad, axis=0)[None]
        term = grad * norms[spots[level] : spots[level] + 1]
        scaled = term if scaled is None else scaled + term
    mean = jnp.mean(scaled, axis=-1, keepdims=True)
    along = jnp.mean(scaled * unit, axis=-1, keepdims=True)
    out[...] = rate * (scaled - mean - unit * along)


def media_back(order, steps):
    shape = jax.ShapeDtypeStruct
    rows, norms, slots = steps[0].media_rows, steps[0].norms, steps[0].slots
    block = pl.BlockSpec((rows.shape[0] // slots, rows.shape[1]), lambda i: (i, 0))

    def whole(array):
        return pl.BlockSpec(array.shape, lambda i: (0, 0))

    spots = [step.spot_m for step in steps]
    pairs = order.all([step.pairs_m for step in steps])
    weights = [step.key_value_w for step in steps]
    grads = pl.pallas_call(
        lambda *refs: media_back_kernel(spots, refs),
        grid=(slots,),
        out_shape=(shape(rows.shape, F32), shape((8, rows.shape[1]), F32)),
        in_specs=[block] * len(steps) + [whole(w) for w in weights] + [block, whole(norms)],
        out_specs=(block, pl.BlockSpec((8, rows.shape[1]), lambda i: (0, 0))),
        cost_estimate=LIGHT,
        name="media_back",
    )(*pairs, *weights, rows, norms)
    return order.gate(*grads)


class Step:
    def __init__(self, lay, order, slots, media_rows, norms, level):
        self.lay, self.order, self.slots = lay, order, slots
        self.media_rows = media_rows
        self.norms = norms
        kinds = 3
        self.gains = [norms[level * kinds + k][None] for k in range(kinds)]
        self.shifts = [norms[(LAYERS + level) * kinds + k][None] for k in range(kinds)]
        self.spot_m = level * kinds
        self.spots = (level * kinds + 2, (LAYERS + level) * kinds + 2)

    def media(self, query_w, key_value_w, output_w):
        self.query_w, self.key_value_w, self.output_w = query_w, key_value_w, output_w
        self.heads = query_w.shape[1] // HEAD
        unit, _ = normalize(self.media_rows.astype(F32))
        self.media_norm = (unit * self.gains[0] + self.shifts[0]).astype(BF16)
        self.own_m = mm(self.media_norm, key_value_w).astype(BF16)
        self.other_m = self.order.send(self.lay.lat.swap, self.own_m)

    def latents(self, rows):
        self.rows = rows
        unit, _ = normalize(rows)
        self.latent_norm = (unit * self.gains[1] + self.shifts[1]).astype(BF16)
        self.own_l = mm(self.latent_norm, self.key_value_w).astype(BF16)
        self.other_l = self.order.send(self.lay.lat.swap, self.own_l)
        self.query = mm(self.latent_norm, self.query_w).astype(BF16)

    def attention(self):
        query, self.other_m, self.other_l = self.order.gate(self.query, self.other_m, self.other_l)
        self.mixed, self.after, self.normed = attend(
            self.slots,
            self.heads,
            self.spots,
            query,
            self.own_m,
            self.other_m,
            self.own_l,
            self.other_l,
            self.rows,
            self.output_w,
            self.norms,
        )

    def feed(self, shared, up_w, down_w):
        self.shared, self.up_w, self.down_w = shared, up_w, down_w
        shared = self.order.gate(shared)
        hidden = mm(shared, up_w)
        big = 0.5 * (1.0 + lax.erf(hidden * (2.0**-0.5)))
        density = jnp.exp(-0.5 * hidden * hidden) * ((2.0 * jnp.pi) ** -0.5)
        self.active = (hidden * big).astype(BF16)
        self.slope = (big + hidden * density).astype(BF16)
        return mm(self.active, down_w).astype(BF16)

    def feed_back(self, branch):
        branch = self.order.gate(branch)
        self.branch = branch
        self.d_hidden = (mm_nt(branch, self.down_w) * self.slope.astype(F32)).astype(BF16)
        return mm_nt(self.d_hidden, self.up_w).astype(BF16)

    def feed_terms(self):
        down = mm_tn(self.active, self.order.gate(self.branch)).astype(BF16)
        up = mm_tn(self.shared, self.d_hidden).astype(BF16)
        rows = up.shape[0] // self.lay.devices
        return FeedGrad(self.lay, self.order, up, down, rows)

    def attention_back(self, normed_grad, upstream):
        normed_grad = self.order.gate(normed_grad)
        (
            self.d_after,
            self.d_query,
            self.d_own_m,
            d_other_m,
            self.d_own_l,
            d_other_l,
            self.output_term,
            self.feed_norm,
        ) = attend_back(
            self.slots,
            self.heads,
            self.spots[0],
            normed_grad,
            upstream,
            self.after,
            self.query,
            (self.own_m, self.other_m, self.own_l, self.other_l),
            self.mixed,
            self.output_w,
            self.norms,
        )
        self.d_other_m, self.d_other_l = d_other_m, d_other_l

    def send_back(self):
        self.back_l = self.order.send(self.lay.lat.swap, self.d_other_l)
        self.back_m = self.order.send(self.lay.lat.swap, self.d_other_m)

    def latents_back(self):
        pairs_l = total(self.order.gate(self.d_own_l, self.back_l)).astype(BF16)
        self.pairs_l = pairs_l
        d_norm = mm_nt(pairs_l, self.key_value_w) + mm_nt(self.d_query, self.query_w)
        d_rows, self.gain_l, self.shift_l = norm_back(d_norm, self.rows, self.gains[1])
        return d_rows + self.d_after

    def attention_terms(self):
        lay = self.lay
        latent_norm = self.order.gate(self.latent_norm)
        width = self.output_w.shape[1]
        half = width // 2
        query = mm_tn(latent_norm, self.d_query).astype(BF16)
        query = query.reshape(lay.devices, -1, half)
        output = self.output_term.reshape(lay.devices, -1, width)
        output = jnp.concatenate([output[..., :half], output[..., half:]], axis=1)
        right = jnp.concatenate([query, output], axis=-1)
        self.pairs_m = total(self.order.gate(self.d_own_m, self.back_m)).astype(BF16)
        pairs_m = self.pairs_m
        left = (mm_tn(self.media_norm, pairs_m) + mm_tn(self.latent_norm, self.pairs_l)).astype(BF16)
        left = left.reshape(lay.devices, -1, width)
        return AttentionGrad(lay, self.order, left, right)

    def norm_terms(self, gain_m, shift_m):
        gains = [gain_m, self.gain_l, self.feed_norm[0]]
        shifts = [shift_m, self.shift_l, self.feed_norm[1]]
        return gains, shifts


def gather_near(lay, order, rows):
    return rows, order.send(lay.tensor[0].swap, rows)


def gather_lat(lay, order, pieces):
    rows = jnp.concatenate(order.all(pieces), axis=0)
    return rows, order.send(lay.lat.swap, rows)


def return_lat(lay, order, rows):
    half = rows.shape[0] // 2
    return rows[:half], order.send(lay.lat.swap, rows[half:])


def return_near(lay, order, terms):
    half = terms[0].shape[0] // 2
    terms = order.all(terms)
    sent = total([term[half:] for term in terms]).astype(BF16)
    return [term[:half] for term in terms] + [order.send(lay.tensor[0].swap, sent)]


def make_device(lay):
    def per_device(
        media_tokens,
        image_counts,
        latent_init,
        cotangent,
        query_weight,
        key_value_weight,
        output_weight,
        up_weight,
        down_weight,
        norm_gain,
        norm_shift,
    ):
        first = norm_gain[0, :1].astype(F32)
        order = Order(first)
        slots = media_tokens.shape[0]
        model = media_tokens.shape[2]
        count = latent_init.shape[0]
        position = jnp.arange(slots) % MEDIA
        per_slot = jnp.repeat(image_counts, MEDIA)
        valid = (position < per_slot).astype(F32)[:, None, None]
        row_mask = jnp.broadcast_to(valid, (slots, count, 1)).reshape(-1, 1)
        media_rows = media_tokens.reshape(-1, model)
        device = lax.axis_index("img") * lax.axis_size("lat") + lax.axis_index("lat")
        lanes = norm_gain.shape[-1]
        kinds = norm_gain.shape[1]
        norms = jnp.concatenate(
            [norm_gain.reshape(-1, lanes), norm_shift.reshape(-1, lanes)], axis=0
        )
        spread = jnp.zeros((NORM_ROWS, model), BF16)
        spread = lax.dynamic_update_slice(spread, norms, (0, device * lanes))
        attn = [
            Attention(
                lay,
                order,
                key_value_weight[level],
                output_weight[level],
                query_weight[level],
                spread if level == 0 else None,
            )
            for level in range(LAYERS)
        ]
        feed = [Feed(lay, order, up_weight[level], down_weight[level]) for level in range(LAYERS)]
        upstream = cotangent.astype(F32).reshape(-1, model) * row_mask

        attn[0].start_column()
        feed[0].start_lat()
        feed[0].start_near()
        attn[0].end_column()
        attn[0].start_plane()
        feed[0].end_near()
        feed[0].start_far()
        feed[1].start_lat()
        feed[1].start_near(attn[1].own)
        feed[1].end_near()
        feed[0].end_far()
        attn[0].end_plane()
        attn[0].start_lat()
        feed[0].start_plane()
        feed[1].start_far()
        weights = attn[0].end_lat()
        step0 = Step(lay, order, slots, media_rows, attn[0].norms, 0)
        step0.media(*weights)
        rows0 = jnp.broadcast_to(latent_init.astype(F32), (slots, count, model)).reshape(-1, model)
        feed[0].next_plane()
        step0.latents(rows0)
        step0.attention()
        pieces = gather_near(lay, order, step0.normed)
        pieces = gather_lat(lay, order, pieces)
        feed_w = feed[0].end_plane()
        attn[1].own = feed[1].end_far()
        attn[1].start_plane()
        out = step0.feed(jnp.concatenate(order.all(pieces), axis=0), *feed_w)
        terms = return_lat(lay, order, out)
        attn[1].end_plane()
        attn[1].start_lat()
        feed[1].start_plane()
        terms = return_near(lay, order, terms)
        weights = attn[1].end_lat()
        step1 = Step(lay, order, slots, media_rows, attn[0].norms, 1)
        step1.media(*weights)
        rows1 = step0.after + total(order.all(terms))
        step1.latents(rows1)
        feed[1].next_plane()
        branch = gather_near(lay, order, upstream.astype(BF16))
        step1.attention()
        pieces = gather_near(lay, order, step1.normed)
        branch = gather_lat(lay, order, branch)
        pieces = gather_lat(lay, order, pieces)
        feed_w = feed[1].end_plane()
        out = step1.feed(jnp.concatenate(order.all(pieces), axis=0), *feed_w)
        terms_out = return_lat(lay, order, out)
        out = step1.feed_back(jnp.concatenate(order.all(branch), axis=0))
        terms = return_lat(lay, order, out)
        feed_grad1 = step1.feed_terms()
        terms = return_near(lay, order, terms)
        feed_grad1.plane(0)
        step1.attention_back(total(order.all(terms)), upstream)
        step1.send_back()
        terms_out = return_near(lay, order, terms_out)
        upstream0 = step1.latents_back()
        branch = gather_near(lay, order, upstream0.astype(BF16))
        feed_grad1.plane(1)
        branch = gather_lat(lay, order, branch)
        attn_grad1 = step1.attention_terms()
        out = step0.feed_back(jnp.concatenate(order.all(branch), axis=0))
        terms = return_lat(lay, order, out)
        attn_grad1.lat()
        terms = return_near(lay, order, terms)
        feed_grad0 = step0.feed_terms()
        attn_grad1.plane(0)
        normed_grad = total(order.all(terms))
        feed_grad1.far()
        feed_grad0.plane(0)
        step0.attention_back(normed_grad, upstream0)
        attn_grad1.settle()
        step0.send_back()
        last = step0.latents_back()
        feed_grad0.plane(1)
        feed_grad1.settle_far()
        attn_grad0 = step0.attention_terms()
        attn_grad0.lat()
        attn_grad1.plane(1)
        feed_grad0.far()
        attn_grad0.plane(0)
        media_grad, norm_m = media_back(order, [step0, step1])
        attn_grad1.settle()
        attn_grad0.settle()
        feed_grad0.settle_far()
        norm_m = order.gate(norm_m)
        gains0, shifts0 = step0.norm_terms(norm_m[0], norm_m[LAYERS])
        gains1, shifts1 = step1.norm_terms(norm_m[1], norm_m[LAYERS + 1])
        small = jnp.stack(gains0 + gains1 + shifts0 + shifts1)
        small = jnp.pad(small, ((0, NORM_ROWS - small.shape[0]), (0, 0)))
        latent = jnp.sum(last.reshape(slots, count, model), axis=0)
        tail = jnp.concatenate([latent, small], axis=0)
        tail = order.gate(tail).astype(BF16)
        tail = [tail, order.send(lay.second.swap, tail)]
        attn_grad1.column_far()
        grads = [feed_grad0, feed_grad1]
        for grad in grads:
            grad.take_far()
        near, lat = lay.tensor
        others = swap_together(lay, order, grads, near, 0)
        attn_grad0.plane(1, total(order.all(tail)))
        take_together(lay, order, grads, near, 0, others)
        others = swap_together(lay, order, grads, lat, 1)
        attn_grad1.column_near()
        attn_grad0.column()
        take_together(lay, order, grads, lat, 1, others)
        end0, tail = attn_grad0.finish()
        for bit in lay.img[4:]:
            tail = tail + order.send(bit.swap, tail)
        small = tail[count:]
        small = small + order.send(lay.lat.swap, small)
        small = lax.dynamic_slice(small, (0, device * lanes), (2 * LAYERS * kinds, lanes))
        ends = [end0, attn_grad1.end()]
        small = small + (order.token - first)
        small = small.reshape(2, LAYERS, kinds, lanes)
        cut = key_value_weight.shape[1]
        lefts = [entry[:cut] for entry in ends]
        rights = [entry[cut:] for entry in ends]
        feeds = [feed_grad0.end(), feed_grad1.end()]
        half = model // 2
        outs = []
        for right in rights:
            cut = right.shape[0] // 2
            outs.append(jnp.concatenate([right[:cut, half:], right[cut:, half:]], axis=1))
        resampled = ((step1.after + total(terms_out)) * row_mask).reshape(cotangent.shape)
        return (
            resampled,
            media_grad.reshape(media_tokens.shape),
            tail[:count],
            jnp.stack([right[:, :half] for right in rights]),
            jnp.stack(lefts),
            jnp.stack(outs),
            jnp.stack([entry[0] for entry in feeds]),
            jnp.stack([entry[1] for entry in feeds]),
            small[0],
            small[1],
        )

    return per_device


def solution(mesh):
    lay = Layout(mesh.shape["img"], mesh.shape["lat"])
    in_specs = (
        P("img", "lat", None),
        P("img"),
        P("lat", None),
        P("img", "lat", None),
        P(None, ("img", "lat"), None),
        P(None, ("img", "lat"), None),
        P(None, ("img", "lat"), None),
        P(None, ("img", "lat"), None),
        P(None, ("img", "lat"), None),
        P(None, None, ("img", "lat")),
        P(None, None, ("img", "lat")),
    )
    out_specs = (
        P("img", "lat", None),
        P("img", "lat", None),
        P("lat", None),
        P(None, ("img", "lat"), None),
        P(None, ("img", "lat"), None),
        P(None, ("img", "lat"), None),
        P(None, ("img", "lat"), None),
        P(None, ("img", "lat"), None),
        P(None, None, ("img", "lat")),
        P(None, None, ("img", "lat")),
    )
    return jax.shard_map(
        make_device(lay), mesh=mesh, in_specs=in_specs, out_specs=out_specs, check_vma=False
    )
```

```python
import jax
import jax.numpy as jnp
from jax import lax
from jax.experimental import pallas as pl
from jax.experimental.pallas import tpu as pltpu
from jax.sharding import PartitionSpec as P

HEAD = 64
MEDIA = 5
LAYERS = 2
F32 = jnp.float32
BF16 = jnp.bfloat16
NORM_ROWS = 16
LIGHT = pl.CostEstimate(flops=1, bytes_accessed=1, transcendentals=0)


class Order:
    def __init__(self, token):
        self.token = token

    def gate(self, *arrays):
        arrays = lax.optimization_barrier(arrays + (self.token,))
        self.token = arrays[-1]
        return arrays[:-1] if len(arrays) > 2 else arrays[0]

    def all(self, arrays):
        arrays = lax.optimization_barrier(tuple(arrays) + (self.token,))
        self.token = arrays[-1]
        return list(arrays[:-1])

    def send(self, swap, array):
        return swap(self.gate(array))


class Bit:
    def __init__(self, axis, size, place, rank):
        self.rank = rank
        self.axis = axis
        self.mask = 1 << place
        self.pairs = [(source, source ^ self.mask) for source in range(size)]

    def mine(self):
        return (lax.axis_index(self.axis) // self.mask) % 2

    def swap(self, array):
        return lax.ppermute(array, self.axis, self.pairs)


class Four:
    def __init__(self, size, place):
        self.shift = 1 << place
        self.swaps = [self._swap(size, mask) for mask in (1, 2, 3)]

    def _swap(self, size, mask):
        pairs = [(source, source ^ (mask * self.shift)) for source in range(size)]
        return lambda array: lax.ppermute(array, "img", pairs)

    def mine(self):
        return (lax.axis_index("img") // self.shift) % 4

    def spread(self, order, array):
        return [order.send(swap, array) for swap in self.swaps]

    def merge(self, own, others, axis):
        pieces = [own] + others
        low = self.mine() % 2 == 0
        high = self.mine() // 2 == 0
        mixed = [
            [jnp.where(low, pieces[2 * a + b], pieces[2 * a + 1 - b]) for b in range(2)]
            for a in range(2)
        ]
        return jnp.stack(
            [jnp.where(high, mixed[c][b], mixed[1 - c][b]) for c in range(2) for b in range(2)],
            axis=axis,
        )

    def add(self, order, array, others):
        array, *others = order.all([array] + others)
        return (array + others[0]) + (others[1] + others[2])

    def shed(self, order, terms, axis):
        me = self.mine()
        terms = list(order.all(terms))
        others = []
        for mask, swap in zip((1, 2, 3), self.swaps):
            sent = total([pick(term, me ^ mask, axis) for term in terms]).astype(BF16)
            others.append(order.send(swap, sent))
        return [pick(term, me, axis) for term in terms] + others


class Layout:
    def __init__(self, img, lat):
        lat_bits = [Bit("lat", lat, k, k) for k in range(lat.bit_length() - 1)]
        img_bits = [Bit("img", img, k, k + len(lat_bits)) for k in range(img.bit_length() - 1)]
        self.devices = img * lat
        self.lat = lat_bits[0]
        self.img = img_bits
        self.every = list(reversed(lat_bits + img_bits))
        self.first, self.second = img_bits[0], img_bits[1]
        self.far = list(reversed(img_bits[3:]))
        self.beyond = list(reversed(img_bits[4:]))
        self.plane = Four(img, 0)
        self.column = Four(img, 2)
        self.tensor = [img_bits[2], lat_bits[0]]
        self.split = 4
        self.outer = img // 16


def pick(array, index, axis):
    return lax.dynamic_index_in_dim(array, index, axis, keepdims=False)


def part(array, bit, place, own):
    return pick(array, bit.mine() if own else 1 - bit.mine(), place)


def pair(bit, own, other, axis):
    low = bit.mine() == 0
    return jnp.stack([jnp.where(low, own, other), jnp.where(low, other, own)], axis=axis)


def join(order, array, bits, have):
    have = list(have)
    for bit in bits:
        other = order.send(bit.swap, array)
        place = sum(1 for held in have if held.rank > bit.rank)
        array = pair(bit, array, other, place)
        have.insert(place, bit)
    return array, have


def total(terms):
    value = terms[0].astype(F32)
    for term in terms[1:]:
        value = value + term.astype(F32)
    return value


def shed(order, terms, bit, have):
    place = have.index(bit)
    terms = order.all(terms)
    sent = total([part(term, bit, place, False) for term in terms]).astype(BF16)
    other = order.send(bit.swap, sent)
    terms = [part(term, bit, place, True) for term in terms] + [other]
    return terms, [held for held in have if held is not bit]


def exchange(order, array, bit, place):
    other = order.send(bit.swap, part(array, bit, place, False))
    return pair(bit, part(array, bit, place, True), other, place)


def mm(a, b):
    return lax.dot_general(a, b, (((1,), (0,)), ((), ())), preferred_element_type=F32)


def mm_nt(a, b):
    return lax.dot_general(a, b, (((1,), (1,)), ((), ())), preferred_element_type=F32)


def mm_tn(a, b):
    return lax.dot_general(a, b, (((0,), (0,)), ((), ())), preferred_element_type=F32)


class Attention:
    def __init__(self, lay, order, kv_shard, out_shard, query_shard, extra):
        self.lay, self.order = lay, order
        self.rows, self.width = kv_shard.shape
        self.out_rows = out_shard.shape[0]
        half = self.width // 2
        outs = jnp.concatenate([out_shard[:, :half], out_shard[:, half:]], axis=0)
        parts = [kv_shard, jnp.concatenate([query_shard, outs], axis=1)]
        if extra is not None:
            parts.append(extra)
        self.extra = extra is not None
        self.own = jnp.concatenate(parts, axis=0)

    def start_column(self):
        lay = self.lay
        self.own, _ = join(self.order, self.own, lay.beyond, [])
        self.own = self.own.reshape((lay.outer,) + self.own.shape[-2:])
        self.others = lay.column.spread(self.order, self.own)

    def end_column(self):
        own, *others = self.order.all([self.own] + self.others)
        self.own = self.lay.column.merge(own, others, 1)

    def start_plane(self):
        self.others = self.lay.plane.spread(self.order, self.own)

    def end_plane(self):
        own, *others = self.order.all([self.own] + self.others)
        self.own = self.lay.plane.merge(own, others, 2)

    def start_lat(self):
        self.others = self.order.send(self.lay.lat.swap, self.own)

    def end_lat(self):
        lay, rows, width = self.lay, self.rows, self.width
        half = width // 2
        self.own, self.others = self.order.gate(self.own, self.others)

        def both(select):
            return pair(lay.lat, select(self.own), select(self.others), 3)

        key_value = both(lambda a: a[..., :rows, :]).reshape(-1, width)
        query = both(lambda a: a[..., rows : 2 * rows, :half]).reshape(-1, half)
        middle = rows + self.out_rows
        output = both(
            lambda a: jnp.concatenate(
                [a[..., rows:middle, half:], a[..., middle : 2 * rows, half:]], axis=-1
            )
        ).reshape(-1, width)
        if self.extra:
            own = self.own[..., 2 * rows :, :].astype(F32)
            other = self.others[..., 2 * rows :, :].astype(F32)
            self.norms = jnp.sum(own, axis=(0, 1, 2)) + jnp.sum(other, axis=(0, 1, 2))
        return query, key_value, output


def feed_columns(lay, array, forward):
    width = array.shape[-1] // lay.devices if forward else None
    ranks = [bit.rank for bit in lay.tensor]
    owner = []
    for device in range(lay.devices):
        value = 0
        for rank in ranks:
            value = value * 2 + (device >> rank) % 2
        owner.append(value)
    if forward:
        blocks = [array[..., d * width : (d + 1) * width] for d in range(lay.devices)]
        sets = [
            jnp.concatenate([blocks[d] for d in range(lay.devices) if owner[d] == s], axis=-1)
            for s in range(lay.split)
        ]
        return jnp.stack(sets)
    width = array.shape[-1] * lay.split // lay.devices
    seen = [0] * lay.split
    blocks = []
    for device in range(lay.devices):
        s = owner[device]
        blocks.append(array[s, :, seen[s] * width : (seen[s] + 1) * width])
        seen[s] += 1
    return jnp.concatenate(blocks, axis=-1)


class Feed:
    def __init__(self, lay, order, up_shard, down_shard):
        self.lay, self.order = lay, order
        self.rows = up_shard.shape[0]
        self.columns = up_shard.shape[1] // lay.split
        up = feed_columns(lay, up_shard, True)
        self.up = up.reshape((2, 2, self.rows, self.columns))
        self.down = down_shard

    def start_lat(self):
        self.other = self.order.send(self.lay.lat.swap, part(self.up, self.lay.lat, 1, False))

    def start_near(self, beside=None):
        self.up, self.other = self.order.gate(self.up, self.other)
        own = part(self.up, self.lay.lat, 1, True)
        self.up = pair(self.lay.lat, own, self.other, 1)
        near = self.lay.tensor[0]
        sent = part(self.up, near, 0, False)
        self.beside = beside
        if beside is not None:
            sent = jnp.concatenate([sent.reshape(-1, self.columns), beside], axis=0)
        self.other = self.order.send(near.swap, sent)

    def end_near(self):
        near = self.lay.tensor[0]
        self.up, self.other = self.order.gate(self.up, self.other)
        own = part(self.up, near, 0, True)
        parts = [pair(near, own, self.other.reshape((-1,) + own.shape[1:])[: own.shape[0]], 0)]
        parts.append(self.down)
        if self.beside is not None:
            cut = own.shape[0] * own.shape[1]
            parts.append(pair(near, self.beside, self.other[cut:], 0))
        self.own = jnp.concatenate([p.reshape(-1, self.columns) for p in parts], axis=0)

    def start_far(self):
        packed, self.have = join(self.order, self.own, self.lay.far[:-1], [])
        self.own = packed
        self.other = self.order.send(self.lay.far[-1].swap, packed)

    def end_far(self):
        place = len(self.have)
        self.own, self.other = self.order.gate(self.own, self.other)
        packed = pair(self.lay.far[-1], self.own, self.other, place)
        self.have = self.have + [self.lay.far[-1]]
        cut = self.rows * self.lay.split
        end = cut + self.down.shape[0]
        up = packed[..., :cut, :]
        self.up = up.reshape((2,) * (len(self.have) + 2) + (self.rows, self.columns))
        self.down = packed[..., cut:end, :]
        if self.beside is not None:
            return packed[..., end:, :].reshape((self.lay.outer, 4) + self.beside.shape)

    def start_plane(self):
        lay = self.lay
        self.up_other = self.order.send(lay.first.swap, self.up)
        self.down_other = self.order.send(lay.second.swap, self.down)

    def gate(self):
        arrays = [self.up, self.up_other, self.down, self.down_other]
        self.up, self.up_other, self.down, self.down_other = self.order.all(arrays)

    def next_plane(self):
        lay = self.lay
        place = len(self.have)
        self.gate()
        self.up = pair(lay.first, self.up, self.up_other, place + 1)
        self.down = pair(lay.second, self.down, self.down_other, place)
        self.up_other = self.order.send(lay.second.swap, self.up)
        self.down_other = self.order.send(lay.first.swap, self.down)

    def end_plane(self):
        lay = self.lay
        place = len(self.have)
        self.gate()
        up = pair(lay.second, self.up, self.up_other, place + 1)
        down = pair(lay.first, self.down, self.down_other, place + 1)
        return up.reshape(-1, self.columns), down.reshape(-1, self.columns)


class FeedGrad:
    def __init__(self, lay, order, up_term, down_term, rows):
        self.lay, self.order, self.rows = lay, order, rows
        self.columns = up_term.shape[1]
        self.up_have = lay.every
        self.up = [up_term.reshape((2,) * len(lay.every) + (rows, self.columns))]
        self.down_have = [bit for bit in lay.every if bit not in lay.tensor]
        self.down = [down_term.reshape((2,) * len(self.down_have) + (-1, self.columns))]

    def plane(self, turn):
        lay = self.lay
        bits = (lay.second, lay.first) if turn == 0 else (lay.first, lay.second)
        self.up, self.up_have = shed(self.order, self.up, bits[0], self.up_have)
        self.down, self.down_have = shed(self.order, self.down, bits[1], self.down_have)

    def settle(self):
        count = len(self.up)
        both = self.order.all(self.up + self.down)
        self.up, self.down = both[:count], both[count:]

    def far(self):
        lay = self.lay
        lead = (2,) * len(lay.far)
        self.settle()
        arrays = [total(self.up), total(self.down)]
        term = jnp.concatenate([a.reshape(lead + (-1, self.columns)) for a in arrays], axis=-2)
        terms, have = [term], list(lay.far)
        for bit in reversed(lay.far):
            terms, have = shed(self.order, terms, bit, have)
        self.terms = terms

    def settle_far(self):
        self.terms = self.order.all(self.terms)

    def take_far(self):
        cut = self.rows * self.lay.split
        packed = total(self.order.all(self.terms))
        self.down = packed[cut:]
        self.up = packed[:cut].astype(BF16).reshape(2, 2, self.rows, self.columns)

    def end(self):
        up = feed_columns(self.lay, self.up.reshape(self.lay.split, self.rows, self.columns), False)
        return up.astype(F32), self.down


def swap_together(lay, order, grads, bit, place):
    sent = jnp.stack([part(grad.up, bit, place, False) for grad in grads])
    return order.send(bit.swap, sent)


def take_together(lay, order, grads, bit, place, others):
    others = order.gate(others)
    for grad, other in zip(grads, others):
        grad.up = pair(bit, part(grad.up, bit, place, True), other, place)


class AttentionGrad:
    def __init__(self, lay, order, left, right):
        self.lay, self.order = lay, order
        self.cut = left.shape[1]
        lead = (lay.outer, 4, 4, 2)
        self.terms = [term.reshape(lead + term.shape[1:]) for term in (left, right)]
        self.tail = None

    def lat(self):
        terms = self.order.all(self.terms)
        lat = self.lay.lat
        sent = jnp.concatenate([part(term, lat, 3, False) for term in terms], axis=-2)
        other = self.order.send(lat.swap, sent)
        own = jnp.concatenate([part(term, lat, 3, True) for term in terms], axis=-2)
        self.terms = [own, other]

    def plane(self, turn, tail=None):
        lay = self.lay
        if turn == 0:
            terms = self.order.all(self.terms)
            width = terms[0].shape[-1]
            cut, rest = self.cut, terms[0].shape[-2] - self.cut
            self.left = [t[..., :cut, :].reshape(-1, 2, 2, cut, width) for t in terms]
            self.right = [t[..., cut:, :].reshape(-1, 2, 2, rest, width) for t in terms]
            places = (1, 2)
        else:
            count = len(self.left)
            terms = self.order.all(self.left + self.right)
            self.left, self.right = terms[:count], terms[count:]
            places = (1, 1)
        bits = (lay.second, lay.first) if turn == 0 else (lay.first, lay.second)
        sent = total([part(term, bits[0], places[0], False) for term in self.left]).astype(BF16)
        own = [part(term, bits[0], places[0], True) for term in self.left]
        if tail is None:
            other = self.order.send(bits[0].swap, sent)
        else:
            tail = tail.astype(BF16)
            rows = sent.size // sent.shape[-1]
            packed = jnp.concatenate([sent.reshape(rows, -1), tail], axis=0)
            packed = self.order.send(bits[0].swap, packed)
            other = packed[:rows].reshape(sent.shape)
            self.tail = [tail, packed[rows:]]
        self.left = own + [other]
        sent = total([part(term, bits[1], places[1], False) for term in self.right]).astype(BF16)
        own = [part(term, bits[1], places[1], True) for term in self.right]
        self.right = own + [self.order.send(bits[1].swap, sent)]

    def join(self):
        count = len(self.left)
        terms = self.order.all(self.left + self.right)
        value = jnp.concatenate([total(terms[:count]), total(terms[count:])], axis=-2)
        return value.reshape((self.lay.outer, 4) + value.shape[-2:])

    def settle(self):
        count = len(self.left)
        terms = self.order.all(self.left + self.right)
        self.left, self.right = terms[:count], terms[count:]

    def column_far(self):
        lay = self.lay
        value = self.join()
        terms, self.have = [value.reshape((2,) * (len(lay.far) + 1) + value.shape[-2:])], lay.far + [lay.tensor[0]]
        for bit in reversed(lay.far):
            terms, self.have = shed(self.order, terms, bit, self.have)
        self.terms = terms

    def column_near(self):
        self.terms, _ = shed(self.order, self.terms, self.lay.tensor[0], self.have)

    def end(self):
        return total(self.order.all(self.terms))

    def column(self):
        value = self.join()
        self.tail = total(self.tail).astype(BF16)
        column = self.lay.column
        me = column.mine()
        self.others = []
        for mask, swap in zip((1, 2, 3), column.swaps):
            sent = pick(value, me ^ mask, 1).astype(BF16)
            sent = jnp.concatenate([sent.reshape(-1, sent.shape[-1]), self.tail], axis=0)
            self.others.append(self.order.send(swap, sent))
        self.own = pick(value, me, 1)

    def finish(self):
        lay = self.lay
        self.own, *others = self.order.all([self.own] + self.others)
        rows = self.own.shape[0] * self.own.shape[1]
        terms = [self.own] + [other[:rows].reshape(self.own.shape) for other in others]
        tails = [self.tail.astype(F32)] + [other[rows:].astype(F32) for other in others]
        tail = (tails[0] + tails[1]) + (tails[2] + tails[3])
        value = total(terms)
        terms = [value.reshape((2,) * len(lay.beyond) + value.shape[1:])]
        have = list(lay.beyond)
        for bit in reversed(lay.beyond):
            terms, have = shed(self.order, terms, bit, have)
        return total(terms), tail


def normalize(rows):
    centered = rows - jnp.mean(rows, axis=-1, keepdims=True)
    rate = lax.rsqrt(jnp.mean(centered * centered, axis=-1, keepdims=True) + 1e-05)
    return centered * rate, rate


def norm_back(grad, rows, gain):
    unit, rate = normalize(rows)
    scaled = grad * gain
    mean = jnp.mean(scaled, axis=-1, keepdims=True)
    along = jnp.mean(scaled * unit, axis=-1, keepdims=True)
    return rate * (scaled - mean - unit * along), jnp.sum(grad * unit, axis=0), jnp.sum(grad, axis=0)


def head_mask(rows, heads, width):
    row = lax.broadcasted_iota(jnp.int32, (heads * rows, width), 0) // rows
    column = lax.broadcasted_iota(jnp.int32, (heads * rows, width), 1) // (width // heads)
    return row == column


def spread_heads(rows, mask, heads):
    return jnp.where(mask, jnp.concatenate([rows] * heads, axis=0), 0)


def merge_heads(array, mask, heads):
    kept = jnp.where(mask, array, 0)
    size = array.shape[0] // heads
    total = kept[:size]
    for head in range(1, heads):
        total = total + kept[head * size : (head + 1) * size]
    return total


def slot_pairs(refs, slot, slots):
    return jnp.concatenate(
        [ref[slot * (ref.shape[0] // slots) : (slot + 1) * (ref.shape[0] // slots)] for ref in refs],
        axis=0,
    )


def soft_scores(query_wide, keys):
    scores = mm_nt(query_wide, keys)
    exponent = jnp.exp(scores - jnp.max(scores, axis=-1, keepdims=True))
    return exponent / jnp.sum(exponent, axis=-1, keepdims=True)


def attend_kernel(slots, heads, spot, refs):
    query, own_m, other_m, own_l, other_l, rows, output_w, norms, mixed, after, normed = refs
    width = query.shape[1]
    count = query.shape[0] // slots
    mask = head_mask(count, heads, width)
    for slot in range(slots):
        pairs = slot_pairs((own_m, other_m, own_l, other_l), slot, slots)
        place = slice(slot * count, (slot + 1) * count)
        wide = spread_heads(query[place] * 0.125, mask, heads)
        probs = soft_scores(wide, pairs[:, :width]).astype(BF16)
        mixed[place] = merge_heads(mm(probs, pairs[:, width:]), mask, heads).astype(BF16)
    total = rows[...] + mm(mixed[...], output_w[...])
    after[...] = total
    unit, _ = normalize(total)
    normed[...] = (unit * norms[spot[0] : spot[0] + 1] + norms[spot[1] : spot[1] + 1]).astype(BF16)


def near_memory(arrays):
    return list(arrays)


def attend(slots, heads, spot, query, own_m, other_m, own_l, other_l, rows, output_w, norms):
    shape = jax.ShapeDtypeStruct
    return pl.pallas_call(
        lambda *refs: attend_kernel(slots, heads, spot, refs),
        out_shape=(
            shape(query.shape, BF16),
            shape(rows.shape, F32),
            shape(rows.shape, BF16),
        ),
        in_specs=[pl.BlockSpec(memory_space=pltpu.VMEM)] * 8,
        out_specs=(pl.BlockSpec(memory_space=pltpu.VMEM),) * 3,
        cost_estimate=LIGHT,
        name="attend",
    )(*near_memory((query, own_m, other_m, own_l, other_l, rows, output_w, norms)))


def attend_back_kernel(slots, heads, spot, refs):
    (
        normed_grad,
        upstream,
        after,
        query,
        own_m,
        other_m,
        own_l,
        other_l,
        mixed,
        output_w,
        norms,
        d_after,
        d_query,
        d_own_m,
        d_other_m,
        d_own_l,
        d_other_l,
        output_grad,
        norm_grad,
        lows,
    ) = refs
    slot = pl.program_id(0)
    width = query.shape[1]
    count = query.shape[0]
    mask = head_mask(count, heads, width)

    @pl.when(slot == 0)
    def _():
        norm_grad[...] = jnp.zeros_like(norm_grad)

    grad, d_gain, d_shift = norm_back(normed_grad[...], after[...], norms[spot : spot + 1])
    grad = grad + upstream[...]
    d_after[...] = grad
    norm_grad[0:1] += d_gain[None]
    norm_grad[1:2] += d_shift[None]
    low = grad.astype(BF16)
    lows[pl.ds(pl.multiple_of(slot * count, count), count)] = low

    @pl.when(slot == slots - 1)
    def _():
        output_grad[...] = mm_tn(mixed[...], lows[...]).astype(BF16)

    mixed_grad = mm_nt(low, output_w[...]).astype(BF16)
    pairs = jnp.concatenate([own_m[...], other_m[...], own_l[...], other_l[...]], axis=0)
    keys, values = pairs[:, :width], pairs[:, width:]
    wide = spread_heads(query[...] * 0.125, mask, heads)
    soft = soft_scores(wide, keys)
    wide_grad = spread_heads(mixed_grad, mask, heads)
    d_probs = mm_nt(wide_grad, values)
    d_values = mm_tn(soft.astype(BF16), wide_grad).astype(BF16)
    d_scores = soft * (d_probs - jnp.sum(d_probs * soft, axis=-1, keepdims=True))
    d_scores = d_scores.astype(BF16)
    d_keys = mm_tn(d_scores, wide).astype(BF16)
    d_query[...] = (merge_heads(mm(d_scores, keys), mask, heads) * 0.125).astype(BF16)
    start = 0
    for ref in (d_own_m, d_other_m, d_own_l, d_other_l):
        size = ref.shape[0]
        ref[:, :width] = d_keys[start : start + size]
        ref[:, width:] = d_values[start : start + size]
        start += size


def attend_back(
    slots, heads, spot, normed_grad, upstream, after, query, pairs, mixed, output_w, norms
):
    shape = jax.ShapeDtypeStruct
    own_m, other_m, own_l, other_l = pairs

    def block(array):
        return pl.BlockSpec((array.shape[0] // slots, array.shape[1]), lambda i: (i, 0))

    def whole(size):
        return pl.BlockSpec(size, lambda i: (0, 0))

    rows = (normed_grad, upstream, after, query, own_m, other_m, own_l, other_l)
    fixed = (mixed, output_w, norms)
    norm_shape = (8, after.shape[1])
    return pl.pallas_call(
        lambda *refs: attend_back_kernel(slots, heads, spot, refs),
        grid=(slots,),
        out_shape=(
            shape(after.shape, F32),
            shape(query.shape, BF16),
            shape(own_m.shape, BF16),
            shape(other_m.shape, BF16),
            shape(own_l.shape, BF16),
            shape(other_l.shape, BF16),
            shape(output_w.shape, BF16),
            shape(norm_shape, F32),
        ),
        in_specs=[block(a) for a in rows] + [whole(a.shape) for a in fixed],
        out_specs=tuple(block(a) for a in (after, query, own_m, other_m, own_l, other_l))
        + (whole(output_w.shape), whole(norm_shape)),
        scratch_shapes=[pltpu.VMEM(after.shape, BF16)],
        cost_estimate=LIGHT,
        name="attend_back",
    )(*rows, *fixed)


def media_back_kernel(spots, refs):
    layers = len(spots)
    pairs, weights = refs[:layers], refs[layers : 2 * layers]
    rows, norms, out, norm_grad = refs[2 * layers :]

    @pl.when(pl.program_id(0) == 0)
    def _():
        norm_grad[...] = jnp.zeros_like(norm_grad)

    unit, rate = normalize(rows[...].astype(F32))
    scaled = None
    for level in range(layers):
        grad = mm_nt(pairs[level][...], weights[level][...])
        norm_grad[level : level + 1] += jnp.sum(grad * unit, axis=0)[None]
        norm_grad[layers + level : layers + level + 1] += jnp.sum(grad, axis=0)[None]
        term = grad * norms[spots[level] : spots[level] + 1]
        scaled = term if scaled is None else scaled + term
    mean = jnp.mean(scaled, axis=-1, keepdims=True)
    along = jnp.mean(scaled * unit, axis=-1, keepdims=True)
    out[...] = rate * (scaled - mean - unit * along)


def media_back(order, steps):
    shape = jax.ShapeDtypeStruct
    rows, norms, slots = steps[0].media_rows, steps[0].norms, steps[0].slots
    block = pl.BlockSpec((rows.shape[0] // slots, rows.shape[1]), lambda i: (i, 0))

    def whole(array):
        return pl.BlockSpec(array.shape, lambda i: (0, 0))

    spots = [step.spot_m for step in steps]
    pairs = order.all([step.pairs_m for step in steps])
    weights = [step.key_value_w for step in steps]
    grads = pl.pallas_call(
        lambda *refs: media_back_kernel(spots, refs),
        grid=(slots,),
        out_shape=(shape(rows.shape, F32), shape((8, rows.shape[1]), F32)),
        in_specs=[block] * len(steps) + [whole(w) for w in weights] + [block, whole(norms)],
        out_specs=(block, pl.BlockSpec((8, rows.shape[1]), lambda i: (0, 0))),
        cost_estimate=LIGHT,
        name="media_back",
    )(*pairs, *weights, rows, norms)
    return order.gate(*grads)


class Step:
    def __init__(self, lay, order, slots, media_rows, norms, level):
        self.lay, self.order, self.slots = lay, order, slots
        self.media_rows = media_rows
        self.norms = norms
        kinds = 3
        self.gains = [norms[level * kinds + k][None] for k in range(kinds)]
        self.shifts = [norms[(LAYERS + level) * kinds + k][None] for k in range(kinds)]
        self.spot_m = level * kinds
        self.spots = (level * kinds + 2, (LAYERS + level) * kinds + 2)

    def media(self, query_w, key_value_w, output_w):
        self.query_w, self.key_value_w, self.output_w = query_w, key_value_w, output_w
        self.heads = query_w.shape[1] // HEAD
        unit, _ = normalize(self.media_rows.astype(F32))
        self.media_norm = (unit * self.gains[0] + self.shifts[0]).astype(BF16)
        self.own_m = mm(self.media_norm, key_value_w).astype(BF16)
        self.other_m = self.order.send(self.lay.lat.swap, self.own_m)

    def latents(self, rows):
        self.rows = rows
        unit, _ = normalize(rows)
        self.latent_norm = (unit * self.gains[1] + self.shifts[1]).astype(BF16)
        self.own_l = mm(self.latent_norm, self.key_value_w).astype(BF16)
        self.other_l = self.order.send(self.lay.lat.swap, self.own_l)
        self.query = mm(self.latent_norm, self.query_w).astype(BF16)

    def attention(self):
        query, self.other_m, self.other_l = self.order.gate(self.query, self.other_m, self.other_l)
        self.mixed, self.after, self.normed = attend(
            self.slots,
            self.heads,
            self.spots,
            query,
            self.own_m,
            self.other_m,
            self.own_l,
            self.other_l,
            self.rows,
            self.output_w,
            self.norms,
        )

    def feed(self, shared, up_w, down_w):
        self.shared, self.up_w, self.down_w = shared, up_w, down_w
        shared = self.order.gate(shared)
        hidden = mm(shared, up_w)
        big = 0.5 * (1.0 + lax.erf(hidden * (2.0**-0.5)))
        density = jnp.exp(-0.5 * hidden * hidden) * ((2.0 * jnp.pi) ** -0.5)
        self.active = (hidden * big).astype(BF16)
        self.slope = (big + hidden * density).astype(BF16)
        return mm(self.active, down_w).astype(BF16)

    def feed_back(self, branch):
        branch = self.order.gate(branch)
        self.branch = branch
        self.d_hidden = (mm_nt(branch, self.down_w) * self.slope.astype(F32)).astype(BF16)
        return mm_nt(self.d_hidden, self.up_w).astype(BF16)

    def feed_terms(self):
        down = mm_tn(self.active, self.order.gate(self.branch)).astype(BF16)
        up = mm_tn(self.shared, self.d_hidden).astype(BF16)
        rows = up.shape[0] // self.lay.devices
        return FeedGrad(self.lay, self.order, up, down, rows)

    def attention_back(self, normed_grad, upstream):
        normed_grad = self.order.gate(normed_grad)
        (
            self.d_after,
            self.d_query,
            self.d_own_m,
            d_other_m,
            self.d_own_l,
            d_other_l,
            self.output_term,
            self.feed_norm,
        ) = attend_back(
            self.slots,
            self.heads,
            self.spots[0],
            normed_grad,
            upstream,
            self.after,
            self.query,
            (self.own_m, self.other_m, self.own_l, self.other_l),
            self.mixed,
            self.output_w,
            self.norms,
        )
        self.d_other_m, self.d_other_l = d_other_m, d_other_l

    def send_back(self):
        self.back_l = self.order.send(self.lay.lat.swap, self.d_other_l)
        self.back_m = self.order.send(self.lay.lat.swap, self.d_other_m)

    def latents_back(self):
        pairs_l = total(self.order.gate(self.d_own_l, self.back_l)).astype(BF16)
        self.pairs_l = pairs_l
        d_norm = mm_nt(pairs_l, self.key_value_w) + mm_nt(self.d_query, self.query_w)
        d_rows, self.gain_l, self.shift_l = norm_back(d_norm, self.rows, self.gains[1])
        return d_rows + self.d_after

    def attention_terms(self):
        lay = self.lay
        latent_norm = self.order.gate(self.latent_norm)
        width = self.output_w.shape[1]
        half = width // 2
        query = mm_tn(latent_norm, self.d_query).astype(BF16)
        query = query.reshape(lay.devices, -1, half)
        output = self.output_term.reshape(lay.devices, -1, width)
        output = jnp.concatenate([output[..., :half], output[..., half:]], axis=1)
        right = jnp.concatenate([query, output], axis=-1)
        self.pairs_m = total(self.order.gate(self.d_own_m, self.back_m)).astype(BF16)
        pairs_m = self.pairs_m
        left = (mm_tn(self.media_norm, pairs_m) + mm_tn(self.latent_norm, self.pairs_l)).astype(BF16)
        left = left.reshape(lay.devices, -1, width)
        return AttentionGrad(lay, self.order, left, right)

    def norm_terms(self, gain_m, shift_m):
        gains = [gain_m, self.gain_l, self.feed_norm[0]]
        shifts = [shift_m, self.shift_l, self.feed_norm[1]]
        return gains, shifts


def gather_near(lay, order, rows):
    return rows, order.send(lay.tensor[0].swap, rows)


def gather_lat(lay, order, pieces):
    rows = jnp.concatenate(order.all(pieces), axis=0)
    return rows, order.send(lay.lat.swap, rows)


def return_lat(lay, order, rows):
    half = rows.shape[0] // 2
    return rows[:half], order.send(lay.lat.swap, rows[half:])


def return_near(lay, order, terms):
    half = terms[0].shape[0] // 2
    terms = order.all(terms)
    sent = total([term[half:] for term in terms]).astype(BF16)
    return [term[:half] for term in terms] + [order.send(lay.tensor[0].swap, sent)]


def make_device(lay):
    def per_device(
        media_tokens,
        image_counts,
        latent_init,
        cotangent,
        query_weight,
        key_value_weight,
        output_weight,
        up_weight,
        down_weight,
        norm_gain,
        norm_shift,
    ):
        first = norm_gain[0, :1].astype(F32)
        order = Order(first)
        slots = media_tokens.shape[0]
        model = media_tokens.shape[2]
        count = latent_init.shape[0]
        position = jnp.arange(slots) % MEDIA
        per_slot = jnp.repeat(image_counts, MEDIA)
        valid = (position < per_slot).astype(F32)[:, None, None]
        row_mask = jnp.broadcast_to(valid, (slots, count, 1)).reshape(-1, 1)
        media_rows = media_tokens.reshape(-1, model)
        device = lax.axis_index("img") * lax.axis_size("lat") + lax.axis_index("lat")
        lanes = norm_gain.shape[-1]
        kinds = norm_gain.shape[1]
        norms = jnp.concatenate(
            [norm_gain.reshape(-1, lanes), norm_shift.reshape(-1, lanes)], axis=0
        )
        spread = jnp.zeros((NORM_ROWS, model), BF16)
        spread = lax.dynamic_update_slice(spread, norms, (0, device * lanes))
        attn = [
            Attention(
                lay,
                order,
                key_value_weight[level],
                output_weight[level],
                query_weight[level],
                spread if level == 0 else None,
            )
            for level in range(LAYERS)
        ]
        feed = [Feed(lay, order, up_weight[level], down_weight[level]) for level in range(LAYERS)]
        upstream = cotangent.astype(F32).reshape(-1, model) * row_mask

        attn[0].start_column()
        feed[0].start_lat()
        feed[0].start_near()
        attn[0].end_column()
        attn[0].start_plane()
        feed[0].end_near()
        feed[0].start_far()
        feed[1].start_lat()
        feed[1].start_near(attn[1].own)
        feed[1].end_near()
        feed[0].end_far()
        attn[0].end_plane()
        attn[0].start_lat()
        feed[0].start_plane()
        feed[1].start_far()
        weights = attn[0].end_lat()
        step0 = Step(lay, order, slots, media_rows, attn[0].norms, 0)
        step0.media(*weights)
        rows0 = jnp.broadcast_to(latent_init.astype(F32), (slots, count, model)).reshape(-1, model)
        feed[0].next_plane()
        step0.latents(rows0)
        step0.attention()
        pieces = gather_near(lay, order, step0.normed)
        pieces = gather_lat(lay, order, pieces)
        feed_w = feed[0].end_plane()
        attn[1].own = feed[1].end_far()
        attn[1].start_plane()
        out = step0.feed(jnp.concatenate(order.all(pieces), axis=0), *feed_w)
        terms = return_lat(lay, order, out)
        attn[1].end_plane()
        attn[1].start_lat()
        feed[1].start_plane()
        terms = return_near(lay, order, terms)
        weights = attn[1].end_lat()
        step1 = Step(lay, order, slots, media_rows, attn[0].norms, 1)
        step1.media(*weights)
        rows1 = step0.after + total(order.all(terms))
        step1.latents(rows1)
        feed[1].next_plane()
        branch = gather_near(lay, order, upstream.astype(BF16))
        step1.attention()
        pieces = gather_near(lay, order, step1.normed)
        branch = gather_lat(lay, order, branch)
        pieces = gather_lat(lay, order, pieces)
        feed_w = feed[1].end_plane()
        out = step1.feed(jnp.concatenate(order.all(pieces), axis=0), *feed_w)
        terms_out = return_lat(lay, order, out)
        out = step1.feed_back(jnp.concatenate(order.all(branch), axis=0))
        terms = return_lat(lay, order, out)
        feed_grad1 = step1.feed_terms()
        terms = return_near(lay, order, terms)
        feed_grad1.plane(0)
        step1.attention_back(total(order.all(terms)), upstream)
        step1.send_back()
        terms_out = return_near(lay, order, terms_out)
        upstream0 = step1.latents_back()
        branch = gather_near(lay, order, upstream0.astype(BF16))
        feed_grad1.plane(1)
        branch = gather_lat(lay, order, branch)
        attn_grad1 = step1.attention_terms()
        out = step0.feed_back(jnp.concatenate(order.all(branch), axis=0))
        terms = return_lat(lay, order, out)
        attn_grad1.lat()
        terms = return_near(lay, order, terms)
        feed_grad0 = step0.feed_terms()
        attn_grad1.plane(0)
        normed_grad = total(order.all(terms))
        feed_grad1.far()
        feed_grad0.plane(0)
        step0.attention_back(normed_grad, upstream0)
        attn_grad1.settle()
        step0.send_back()
        last = step0.latents_back()
        feed_grad0.plane(1)
        feed_grad1.settle_far()
        attn_grad0 = step0.attention_terms()
        attn_grad0.lat()
        attn_grad1.plane(1)
        feed_grad0.far()
        attn_grad0.plane(0)
        media_grad, norm_m = media_back(order, [step0, step1])
        attn_grad1.settle()
        attn_grad0.settle()
        feed_grad0.settle_far()
        norm_m = order.gate(norm_m)
        gains0, shifts0 = step0.norm_terms(norm_m[0], norm_m[LAYERS])
        gains1, shifts1 = step1.norm_terms(norm_m[1], norm_m[LAYERS + 1])
        small = jnp.stack(gains0 + gains1 + shifts0 + shifts1)
        small = jnp.pad(small, ((0, NORM_ROWS - small.shape[0]), (0, 0)))
        latent = jnp.sum(last.reshape(slots, count, model), axis=0)
        tail = jnp.concatenate([latent, small], axis=0)
        tail = order.gate(tail).astype(BF16)
        tail = [tail, order.send(lay.second.swap, tail)]
        attn_grad1.column_far()
        grads = [feed_grad0, feed_grad1]
        for grad in grads:
            grad.take_far()
        near, lat = lay.tensor
        others = swap_together(lay, order, grads, near, 0)
        attn_grad0.plane(1, total(order.all(tail)))
        take_together(lay, order, grads, near, 0, others)
        others = swap_together(lay, order, grads, lat, 1)
        attn_grad1.column_near()
        attn_grad0.column()
        take_together(lay, order, grads, lat, 1, others)
        end0, tail = attn_grad0.finish()
        for bit in lay.img[4:]:
            tail = tail + order.send(bit.swap, tail)
        small = tail[count:]
        small = small + order.send(lay.lat.swap, small)
        small = lax.dynamic_slice(small, (0, device * lanes), (2 * LAYERS * kinds, lanes))
        ends = [end0, attn_grad1.end()]
        small = small + (order.token - first)
        small = small.reshape(2, LAYERS, kinds, lanes)
        cut = key_value_weight.shape[1]
        lefts = [entry[:cut] for entry in ends]
        rights = [entry[cut:] for entry in ends]
        feeds = [feed_grad0.end(), feed_grad1.end()]
        half = model // 2
        outs = []
        for right in rights:
            cut = right.shape[0] // 2
            outs.append(jnp.concatenate([right[:cut, half:], right[cut:, half:]], axis=1))
        resampled = ((step1.after + total(terms_out)) * row_mask).reshape(cotangent.shape)
        return (
            resampled,
            media_grad.reshape(media_tokens.shape),
            tail[:count],
            jnp.stack([right[:, :half] for right in rights]),
            jnp.stack(lefts),
            jnp.stack(outs),
            jnp.stack([entry[0] for entry in feeds]),
            jnp.stack([entry[1] for entry in feeds]),
            small[0],
            small[1],
        )

    return per_device


def solution(mesh):
    lay = Layout(mesh.shape["img"], mesh.shape["lat"])
    in_specs = (
        P("img", "lat", None),
        P("img"),
        P("lat", None),
        P("img", "lat", None),
        P(None, ("img", "lat"), None),
        P(None, ("img", "lat"), None),
        P(None, ("img", "lat"), None),
        P(None, ("img", "lat"), None),
        P(None, ("img", "lat"), None),
        P(None, None, ("img", "lat")),
        P(None, None, ("img", "lat")),
    )
    out_specs = (
        P("img", "lat", None),
        P("img", "lat", None),
        P("lat", None),
        P(None, ("img", "lat"), None),
        P(None, ("img", "lat"), None),
        P(None, ("img", "lat"), None),
        P(None, ("img", "lat"), None),
        P(None, ("img", "lat"), None),
        P(None, None, ("img", "lat")),
        P(None, None, ("img", "lat")),
    )
    return jax.shard_map(
        make_device(lay), mesh=mesh, in_specs=in_specs, out_specs=out_specs, check_vma=False
    )
```
